32 devices in a mesh: sub: 4 (over z), wide: 8 (over y, x, core).
Axes of the slice: x: 2, y: 2, z: 4, core: 2. Of those that a mesh axis runs over, the one named last changes fastest.
Arguments:
- load_table: bfloat16 [4, 8, 16, 4, 128], P('sub', 'wide'), may hold values from -6 to 6
- load_column: int32 [64], replicated, may hold values from 0 to 15
- face_order: int32 [4, 8, 4], P('sub', 'wide'), may hold values from 0 to 3, each once within a row
- schur: bfloat16 [4, 8, 512, 512], P('sub', 'wide'), as said below
- neumann: bfloat16 [4, 8, 512, 512], P('sub', 'wide'), as said below
- coarse_basis: bfloat16 [4, 8, 4, 4, 128], P('sub', 'wide'), may hold values from -0.625 to 0.625
- corner_map: int32 [4, 8, 4], P('sub', 'wide'), may hold values from 0 to 47, as said below
- coarse_inverse: float32 [48, 48], P('wide'), as said below
Outputs:
- solution: float32 [4, 8, 4, 64, 128], P('sub', 'wide')
The draws below stay inside these ranges and needn't reach their ends.
Inputs may be any that keep to these rules, and one draw needn't show every extreme that they name: `corner_map`: each subdomain's 4 entries are distinct; subdomains that meet at a corner of the grid of subdomains give it the same number, and different corners get different numbers, so (5) * (9) of the 48 numbers occur and the others belong to no corner. `coarse_inverse`: Symmetric. `schur`: Symmetric. `neumann`: Symmetric.
All inputs are finite; a program needn't handle non-finite values.
Results may differ from the reference program's by a relative error of at most 0.0014.
Values sent between devices are 32-bit elements; how exact they have to be, the bound alone decides.
A program may use at most 64 MiB of HBM per device.

```python
import math
import jax
import jax.numpy as jnp
from jax import lax

NI = 512
RHS = 64
NLOAD = 16
PRIM = 4
ITERS = 3
FB = 128
ROWS = 4
COLS = 8
NCOARSE = 48


def spd_blocks(key, lowest, highest, spread):
    key_diag, key_noise = jax.random.split(key)
    diagonal = jax.random.uniform(key_diag, (ROWS, COLS, NI), jnp.float32, lowest, highest)
    noise_part = jax.random.normal(key_noise, (ROWS, COLS, NI, NI), jnp.float32) * (spread / math.sqrt(2.0 * NI))
    symmetric = noise_part + jnp.swapaxes(noise_part, 2, 3)
    identity = jnp.eye(NI, dtype=jnp.float32)
    return (symmetric + diagonal[..., None] * identity).astype(jnp.bfloat16)


def draw_schur(key, part):
    return spd_blocks(jax.random.fold_in(key, 11), 1.0, 2.0, 0.35)


def draw_neumann(key, part):
    return spd_blocks(jax.random.fold_in(key, 23), 0.6, 1.2, 0.25)


def draw_coarse_inverse(key, part):
    key_diag, key_noise = jax.random.split(jax.random.fold_in(key, 37))
    lowest, highest, spread = (0.6, 1.2, 0.2)
    diagonal = jax.random.uniform(key_diag, (NCOARSE,), jnp.float32, lowest, highest)
    noise_part = jax.random.normal(key_noise, (NCOARSE, NCOARSE), jnp.float32) * (spread / math.sqrt(1.0 * NCOARSE))
    symmetric = noise_part + noise_part.T
    return symmetric + jnp.diag(diagonal)


def draw_corner_map(key, part):
    numbering = jax.random.permutation(jax.random.fold_in(key, 53), NCOARSE)
    corner_base = jnp.arange(ROWS)[:, None] * (COLS + 1) + jnp.arange(COLS)[None, :]
    corner_index = jnp.stack([corner_base, corner_base + 1, corner_base + COLS + 1, corner_base + COLS + 2], axis=-1)
    return numbering[corner_index].astype(jnp.int32)


def place_ends(array, stream_key, low, top_value):
    longest = array.shape.index(max(array.shape))
    spots = []
    for shift in (0, 1):
        where = [jax.random.randint(jax.random.fold_in(stream_key, axis), (), 0, length) for axis, length in enumerate(array.shape)]
        where[longest] = (where[longest] + shift) % array.shape[longest]
        spots.append(tuple(where))
    return array.at[spots[0]].set(low).at[spots[1]].set(top_value)


def level_of(stream_key, shape, cuts, smallest, largest):
    def one(position, shards_of):
        draws = jax.random.uniform(jax.random.fold_in(jax.random.fold_in(stream_key, 6), position), (shards_of,), jnp.float32, smallest / len(cuts), largest / len(cuts))
        return jnp.repeat(jnp.exp(draws), shape[position] // shards_of).reshape((-1,) + (1,) * (len(shape) - position - 1))

    gain = one(*cuts[0])
    for cut in cuts[1:]:
        gain = gain * one(*cut)
    return gain


def noise(stream_key, shape, scale, bound, cuts=(), kind=jnp.bfloat16):
    drawn = scale * jax.random.normal(stream_key, shape, jnp.float32)
    if cuts:
        drawn = drawn * level_of(stream_key, shape, cuts, -0.22, 0.18)
    return jnp.clip(drawn, -bound, bound).astype(kind)


def setup_inputs(seed: int = 0) -> dict:
    key_list = jax.random.split(jax.random.key(seed), 9)
    load_table = noise(key_list[0], (ROWS, COLS, NLOAD, 4, FB), 1.0, 6.0, ((0, 4), (1, 8)))
    load_column = place_ends(jax.random.randint(key_list[1], (RHS,), 0, NLOAD), jax.random.fold_in(key_list[1], 1), 0, NLOAD - 1).astype(jnp.int32)
    face_order = jax.vmap(lambda own: jax.random.permutation(own, 4))(jax.random.split(key_list[2], ROWS * COLS)).reshape((ROWS, COLS, 4)).astype(jnp.int32)
    schur = draw_schur(jax.random.fold_in(key_list[8], 71), 0)
    neumann = draw_neumann(jax.random.fold_in(key_list[8], 71), 0)
    coarse_basis = noise(key_list[5], (ROWS, COLS, PRIM, 4, FB), (NI // 5) ** -0.5, 0.625, ((0, 4), (1, 8)))
    corner_map = draw_corner_map(jax.random.fold_in(key_list[8], 71), 0)
    coarse_inverse = draw_coarse_inverse(jax.random.fold_in(key_list[8], 71), 0)
    return dict(load_table=load_table, load_column=load_column, face_order=face_order, schur=schur, neumann=neumann, coarse_basis=coarse_basis, corner_map=corner_map, coarse_inverse=coarse_inverse)


damping = 0.3


def share_weights():
    row_index = jnp.arange(ROWS)[:, None] * jnp.ones((1, COLS), jnp.int32)
    col_index = jnp.ones((ROWS, 1), jnp.int32) * jnp.arange(COLS)[None, :]
    half = jnp.float32(0.5)
    whole = jnp.float32(1.0)
    north_share = jnp.where(row_index > 0, half, whole)
    south_share = jnp.where(row_index < ROWS - 1, half, whole)
    west_share = jnp.where(col_index > 0, half, whole)
    east_share = jnp.where(col_index < COLS - 1, half, whole)
    return jnp.stack([north_share, south_share, west_share, east_share], axis=2)[:, :, :, None, None]


def assemble(copies):
    empty_row = jnp.zeros_like(copies[:1, :, 0])
    empty_col = jnp.zeros_like(copies[:, :1, 0])
    upper_faces = jnp.concatenate([empty_row, copies[:-1, :, 1]], axis=0)
    lower_faces = jnp.concatenate([copies[1:, :, 0], empty_row], axis=0)
    left_faces = jnp.concatenate([empty_col, copies[:, :-1, 3]], axis=1)
    right_faces = jnp.concatenate([copies[:, 1:, 2], empty_col], axis=1)
    return jnp.stack([copies[:, :, 0] + upper_faces, copies[:, :, 1] + lower_faces,
                      copies[:, :, 2] + left_faces, copies[:, :, 3] + right_faces], axis=2)


def apply_local(vectors, operators, face_order):
    selector = (face_order[..., :, None] == jnp.arange(4, dtype=jnp.int32)).astype(jnp.float32)
    rounded = lax.optimization_barrier(vectors.astype(jnp.bfloat16)).astype(jnp.float32)
    blocked = jnp.einsum('rcbf,rcfjn->rcjbn', selector, rounded, precision=lax.Precision.HIGHEST)
    blocked = blocked.reshape(ROWS * COLS, RHS, NI).astype(jnp.bfloat16)
    flat_ops = operators.reshape(ROWS * COLS, NI, NI)
    product = lax.map(lambda operands: jnp.dot(operands[0], operands[1], preferred_element_type=jnp.float32),
                      (blocked, flat_ops))
    product = product.reshape(ROWS, COLS, RHS, 4, FB)
    return jnp.einsum('rcbf,rcjbn->rcfjn', selector, product, precision=lax.Precision.HIGHEST)


def reference(load_table, load_column, face_order, schur, neumann, coarse_basis, corner_map, coarse_inverse):
    load_select = (load_column[:, None] == jnp.arange(NLOAD, dtype=jnp.int32)).astype(jnp.float32)
    load_faces = jnp.einsum('jl,rclfn->rcfjn', load_select, load_table.astype(jnp.float32),
                            precision=lax.Precision.HIGHEST)
    weights = share_weights()
    basis = coarse_basis.astype(jnp.float32)
    solution = jnp.zeros((ROWS, COLS, 4, RHS, FB), jnp.float32)
    for iteration in range(ITERS):
        if iteration == 0:
            residual = assemble(load_faces)
        else:
            residual = assemble(load_faces - apply_local(solution, schur, face_order))
        weighted = weights * residual
        restricted = jnp.einsum('rcpfn,rcfjn->rcpj', basis, weighted, precision=lax.Precision.HIGHEST)
        coarse_residual = jax.ops.segment_sum(restricted.reshape(ROWS * COLS * PRIM, RHS),
                                              corner_map.reshape(ROWS * COLS * PRIM), NCOARSE)
        coarse_solution = jnp.dot(coarse_residual.T, coarse_inverse, precision=lax.Precision.HIGHEST)
        picked = coarse_solution[:, corner_map]
        correction = jnp.einsum('jrcp,rcpfn->rcfjn', picked, basis, precision=lax.Precision.HIGHEST)
        neumann_part = apply_local(weighted, neumann, face_order)
        update = assemble(weights * (neumann_part + correction))
        solution = solution + damping * update
    return solution
```

```python
import functools

import jax
import jax.numpy as jnp
from jax import lax
from jax.experimental import pallas as pl
from jax.experimental.pallas import tpu as pltpu
from jax.sharding import PartitionSpec as P

ITERS = 3
damping = 0.3
MESH = pl.DeviceIdType.MESH
HIGHEST = lax.Precision.HIGHEST
OPPOSITE = (1, 0, 3, 2)
MARK = 16
VMEM_LIMIT = 56 * 1024 * 1024


def split(value):
    high = value.astype(jnp.bfloat16)
    low = (value - high.astype(jnp.float32)).astype(jnp.bfloat16)
    return high, low


def split3(value):
    high, low = split(value)
    rest = value - high.astype(jnp.float32) - low.astype(jnp.float32)
    return high, low, rest.astype(jnp.bfloat16)


def dot(a, b, dims=((1,), (0,)), precision=None):
    return lax.dot_general(
        a, b, (dims, ((), ())), precision=precision, preferred_element_type=jnp.float32
    )


def kernel(
    sizes,
    face_order_hbm,
    corner_map_hbm,
    load_table_hbm,
    basis_hbm,
    inverse_hbm,
    column_hbm,
    schur_hbm,
    neumann_hbm,
    out,
    face_order,
    corner_map,
    load_table,
    basis_in,
    inverse_in,
    column,
    schur_in,
    neumann_in,
    schur,
    neumann,
    load,
    sol,
    face_out,
    face_in,
    basis_out,
    basis_near,
    inverse_all,
    inverse_flat,
    corner_flat,
    gmat,
    hot,
    chosen,
    coarse,
    coarse_out,
    coarse_near,
    rest_all,
    rest_flat,
    far_sem,
    local_sem,
    block_sem,
    face_send,
    face_recv,
    basis_send,
    basis_recv,
    coarse_send,
    coarse_recv,
    inverse_send,
    inverse_recv,
    rest_send,
    rest_recv,
):
    subs, wides = sizes
    devices = subs * wides
    rhs, width = load.shape[1], load.shape[2]
    inner = 4 * width
    prims = basis_out.shape[1] // 2
    order = inverse_flat.shape[0]
    owned = inverse_in.shape[0]
    used = 5 * rhs
    small_mesh = devices <= 32
    row = lax.axis_index("sub")
    col = lax.axis_index("wide")
    me = row * wides + col
    has = (row > 0, row < subs - 1, col > 0, col < wides - 1)
    near = ((row - 1, col), (row + 1, col), (row, col - 1), (row, col + 1))
    share = [jnp.where(flag, jnp.float32(0.5), jnp.float32(1.0)) for flag in has]
    faces = range(4)

    pairs = (
        (load_table_hbm, load_table),
        (basis_hbm, basis_in),
        (corner_map_hbm, corner_map),
        (face_order_hbm, face_order),
        (inverse_hbm, inverse_in),
        (column_hbm, column),
    )
    fetch = [
        pltpu.make_async_copy(source, target, local_sem.at[i])
        for i, (source, target) in enumerate(pairs)
    ]
    blocks = [
        [
            pltpu.make_async_copy(
                source.at[:, :, b * width : (b + 1) * width], target.at[b], sems.at[b]
            )
            for b in faces
        ]
        for source, target, sems in (
            (neumann_hbm, neumann_in, block_sem.at[0]),
            (schur_hbm, schur_in, block_sem.at[1]),
        )
    ]
    for copy in fetch[:3]:
        copy.start()

    def loop(first, last, action):
        if small_mesh:
            for step in range(first, last):
                action(step)
        else:

            def one(step, carry):
                action(step)
                return carry

            lax.fori_loop(first, last, one, 0)

    def each_wide(action):
        loop(1, wides, lambda step: action(lax.rem(col + step, wides)))

    def each_sub(action):
        loop(1, subs, lambda step: action(lax.rem(row + step, subs)))

    barrier = pltpu.get_barrier_semaphore()

    def signal(sem, where):
        pl.semaphore_signal(sem, inc=1, device_id=where, device_id_type=MESH)

    each_sub(lambda other: signal(barrier, (other, col)))
    each_wide(lambda other: signal(barrier, (row, other)))
    for copy in fetch[3:] + blocks[0] + blocks[1]:
        copy.start()

    def face_copy(turn, f):
        return pltpu.make_async_remote_copy(
            src_ref=face_out.at[turn, f],
            dst_ref=face_in.at[turn, OPPOSITE[f]],
            send_sem=face_send.at[turn, f],
            recv_sem=face_recv.at[turn, OPPOSITE[f]],
            device_id=near[f],
            device_id_type=MESH,
        )

    def to_near(source, target, send, recv, f):
        return pltpu.make_async_remote_copy(
            src_ref=source.at[f],
            dst_ref=target.at[OPPOSITE[f]],
            send_sem=send.at[f],
            recv_sem=recv.at[OPPOSITE[f]],
            device_id=near[f],
            device_id_type=MESH,
        )

    def basis_copy(f):
        return to_near(basis_out, basis_near, basis_send, basis_recv, f)

    def coarse_copy(f):
        return to_near(coarse_out, coarse_near, coarse_send, coarse_recv, f)

    def inverse_copy(other):
        return pltpu.make_async_remote_copy(
            src_ref=inverse_all.at[col],
            dst_ref=inverse_all.at[col],
            send_sem=inverse_send.at[other],
            recv_sem=inverse_recv.at[col],
            device_id=(row, other),
            device_id_type=MESH,
        )

    def rest_copy(iteration, where):
        return pltpu.make_async_remote_copy(
            src_ref=rest_all.at[iteration, me],
            dst_ref=rest_all.at[iteration, me],
            send_sem=rest_send.at[iteration],
            recv_sem=rest_recv.at[iteration],
            device_id=where,
            device_id_type=MESH,
        )

    def each_near(action):
        for f in faces:

            @pl.when(has[f])
            def _():
                action(f)

    def wait_near(target, recv):
        each_near(lambda f: pltpu.make_async_copy(target.at[f], target.at[f], recv.at[f]).wait())

    def wait_others(blocks, sem):
        others = blocks.at[pl.ds(0, devices - 1)]
        pltpu.make_async_copy(others, others, sem).wait()

    def send_faces(turn):
        each_near(lambda f: face_copy(turn, f).start())

    def wait_faces(turn):
        wait_near(face_in.at[turn], face_recv.at[turn])

    def drain_faces(turn):
        each_near(lambda f: face_copy(turn, f).wait_send())

    upper = row < (subs + 1) // 2
    half = subs // 2

    def send_rest(iteration, first, last):
        def rows(i):
            there = jnp.where(upper, subs - 1 - i, i)

            def columns(step):
                other = lax.rem(col + step, wides)

                def start():
                    rest_copy(iteration, (there, other)).start()

                if isinstance(step, int) and step > 0:
                    start()
                elif isinstance(step, int) and isinstance(i, int) and i < half:
                    start()
                else:
                    pl.when(jnp.logical_or(there != row, step != 0))(start)

            loop(0, wides, columns)

        loop(first, last, rows)

    def side(values):
        return jnp.concatenate(values, axis=1)

    def cut(value):
        return [value[:, f * width : (f + 1) * width] for f in faces]

    def arranged(rows):
        target = 4 * lax.broadcasted_iota(jnp.int32, (rows, 4 * rows), 0)
        source = lax.broadcasted_iota(jnp.int32, (rows, 4 * rows), 1)
        picks = [(source == target + f).astype(jnp.float32) for f in faces]
        return jnp.concatenate(picks, axis=0).astype(jnp.bfloat16)

    table_picks = arranged(rhs)
    basis_picks = arranged(prims)
    weights = side([share[f] * jnp.ones((1, width), jnp.float32) for f in faces])

    fetch[0].wait()
    table = dot(table_picks, load_table[...])
    for f in faces:
        load[f] = table[f * rhs : (f + 1) * rhs]
        face_out[0, f] = table[f * rhs : (f + 1) * rhs]
    fetch[1].wait()
    fetch[2].wait()
    own = dot(basis_picks, basis_in[...])
    row_of = lax.broadcasted_iota(jnp.int32, (prims, width), 0)
    marks = jnp.zeros((prims, width), jnp.int32)
    for p in range(prims):
        marks = jnp.where(row_of == p, corner_map[p], marks)
    marks = marks.astype(jnp.float32)
    for f in faces:
        basis_out[f] = jnp.concatenate([own[f * prims : (f + 1) * prims], marks], axis=0)

    pl.semaphore_wait(barrier, subs - 1 + wides - 1)
    send_faces(0)
    each_near(lambda f: basis_copy(f).start())
    each_wide(lambda other: signal(far_sem, (row, other)))
    fetch[4].wait()
    inverse_all[col] = inverse_in[...]
    each_wide(lambda other: inverse_copy(other).start())

    for f in faces:

        @pl.when(jnp.logical_not(has[f]))
        def _():
            for turn in range(2 * ITERS):
                face_in[turn, f] = jnp.zeros((rhs, width), jnp.float32)
            basis_near[f] = jnp.zeros(basis_near.shape[1:], jnp.float32)
            coarse_near[f] = jnp.zeros(coarse_near.shape[1:], jnp.float32)

    fetch[3].wait()
    spot = []
    for f in faces:
        found = jnp.int32(0)
        for b in range(1, 4):
            found = jnp.where(face_order[b] == f, jnp.int32(b), found)
        spot.append(found)

    def by_face(source, target):
        for f in faces:
            for g in faces:
                target[f * width : (f + 1) * width, g * width : (g + 1) * width] = source[
                    spot[g], spot[f]
                ]

    for copy in blocks[0]:
        copy.wait()
    by_face(neumann_in, neumann)

    def weighted(turn):
        return side([share[f] * (face_out[turn, f] + face_in[turn, f]) for f in faces])

    def apply_neumann(turn, values):
        result = dot(values.astype(jnp.bfloat16), neumann[...])
        for f, part in enumerate(cut(result)):
            face_out[turn, f] = part
        send_faces(turn)

    wait_faces(0)
    apply_neumann(1, weighted(0))

    wait_near(basis_near, basis_recv)
    gmat[...] = jnp.zeros(gmat.shape, jnp.float32)
    gmat[0:prims, :] = side([basis_out[f, :prims] for f in faces])
    for f in faces:
        gmat[(f + 1) * prims : (f + 2) * prims, f * width : (f + 1) * width] = basis_near[
            f, :prims
        ]
    shared = (gmat[...] * weights).astype(jnp.bfloat16)

    def restrict(iteration, values):
        high, low = split(values)
        both = dot(shared, jnp.concatenate([high, low], axis=0), ((1,), (1,)))
        parts = both[:, :rhs] + both[:, rhs:]
        rows = [parts[g * prims : (g + 1) * prims] for g in range(5)]
        rest_all[iteration, me] = side(rows + [marks[:, :MARK]])

    restrict(0, side([load[f] for f in faces]))
    pl.semaphore_wait(far_sem, wides - 1)
    send_rest(0, 0, subs)

    for copy in blocks[1]:
        copy.wait()
    by_face(schur_in, schur)
    each_wide(
        lambda other: pltpu.make_async_copy(
            inverse_all.at[other], inverse_all.at[other], inverse_recv.at[other]
        ).wait()
    )
    for w in range(wides):
        inverse_flat[w * owned : (w + 1) * owned, :] = inverse_all[w]
    lanes = lax.broadcasted_iota(jnp.int32, (prims, order), 1).astype(jnp.float32)
    picks = [marks[:, :1] == lanes]
    picks += [basis_near[f, prims:, :1] == lanes for f in faces]
    mine = jnp.concatenate([flag.astype(jnp.float32) for flag in picks], axis=0)
    dense = dot(mine.T.astype(jnp.bfloat16), gmat[...].astype(jnp.bfloat16))
    spread = damping * weights * dot(inverse_flat[...], dense, ((1,), (0,)), HIGHEST)
    high, low = split(spread)
    coarse[0, :, :inner], coarse[1, :, :inner] = high, low
    both = dot(jnp.concatenate([high, low], axis=0), schur[...])
    effect = both[:order] + both[order:]
    high, low = split(effect)
    coarse[0, :, inner : 2 * inner], coarse[1, :, inner : 2 * inner] = high, low
    for f, part in enumerate(cut(effect)):
        coarse_out[f] = part
    each_near(lambda f: coarse_copy(f).start())

    def apply_schur(turn, values):
        high, low = split(values)
        both = dot(jnp.concatenate([high, low], axis=0), schur[...])
        for f, part in enumerate(cut(both[:rhs] + both[rhs:])):
            face_out[turn, f] = load[f] - part
        send_faces(turn)

    group = min(devices, 32)
    span = group * prims
    shifts = (0, -wides, wides, -1, 1)

    def mark(part):
        for g in range(5):
            for d in range(group):
                peer = jnp.clip(part * group + d + shifts[g], 0, devices - 1)
                start = g * span + d * prims
                corner_flat[start : start + prims, :] = rest_all[0, peer][:, used:]
        lanes = lax.broadcasted_iota(jnp.int32, hot.shape, 1).astype(jnp.float32)
        hot[...] = (corner_flat[:, :1] == lanes).astype(jnp.float32).astype(jnp.bfloat16)

    def gather(iteration):
        def one(part):
            if devices > group:
                mark(part)
            for d in range(group):
                rest_flat[d * prims : (d + 1) * prims, :] = rest_all[
                    iteration, part * group + d
                ][:, :used]
            turned = rest_flat[...].T
            lined = side([turned[g * rhs : (g + 1) * rhs] for g in range(5)])
            high, low = split(lined)
            both = dot(jnp.concatenate([high, low], axis=0), hot[...])
            return both[:rhs] + both[rhs:]

        wait_others(rest_all.at[iteration], rest_recv.at[iteration])
        if devices == group:
            if iteration == 0:
                mark(0)
            return one(0)
        return lax.fori_loop(
            0,
            devices // group,
            lambda part, total: total + one(part),
            jnp.zeros((rhs, order), jnp.float32),
        )

    def correct(iteration, columns):
        high, low = split(gather(iteration))
        both = dot(jnp.concatenate([high, low], axis=0), coarse[0, :, :columns])
        return both[:rhs] + both[rhs:] + dot(high, coarse[1, :, :columns])

    def expand(values):
        return dot(chosen[...], jnp.concatenate(split3(values), axis=0))

    scaled = damping * weights

    def advanced(turn, base):
        change = scaled * side([face_out[turn, f] + face_in[turn, f] for f in faces])
        return change if base is None else base + change

    drain_faces(0)
    each_near(lambda f: basis_copy(f).wait_send())
    wait_faces(1)
    sol[...] = advanced(1, None)

    for iteration in range(1, ITERS):
        first = 2 * iteration
        last = iteration == ITERS - 1
        apply_schur(first, sol[...])
        if iteration == 1:
            wait_near(coarse_near, coarse_recv)
            joined = [coarse_out[f] + coarse_near[f] for f in faces]
            high, low = split(weights * side(joined))
            coarse[0, :, 2 * inner :], coarse[1, :, 2 * inner :] = high, low
            fetch[5].wait()
            wanted = lax.broadcasted_iota(jnp.int32, (rhs, column.shape[1]), 0) == column[...]
            wanted = wanted.astype(jnp.float32).T.astype(jnp.bfloat16)
            chosen[...] = side([wanted, wanted, wanted])
        change = correct(iteration - 1, 3 * inner)
        local = side([face_out[first, f] for f in faces])
        restrict(iteration, local - change[:, inner : 2 * inner])
        send_rest(iteration, 0, half)
        sol[...] += change[:, :inner]
        wait_faces(first)
        apply_neumann(first + 1, weighted(first) - change[:, 2 * inner :])
        send_rest(iteration, half, subs)
        drain_faces(first - 1)
        drain_faces(first)
        if last:
            change = correct(iteration, inner)
            for f, part in enumerate(cut(expand(sol[...] + change))):
                out[f] = part
            wait_faces(first + 1)
            for f, part in enumerate(cut(expand(advanced(first + 1, None)))):
                out[f] = out[f] + part
        else:
            wait_faces(first + 1)
            sol[...] = advanced(first + 1, sol[...])

    drain_faces(2 * ITERS - 1)
    each_near(lambda f: coarse_copy(f).wait_send())
    each_wide(lambda other: inverse_copy(other).wait_send())
    for iteration in range(ITERS):
        wait_others(rest_all.at[iteration], rest_send.at[iteration])


def body(
    load_table, load_column, face_order, schur, neumann, coarse_basis, corner_map, coarse_inverse
):
    subs, wides = lax.axis_size("sub"), lax.axis_size("wide")
    devices = subs * wides
    patterns, width = load_table.shape[2], load_table.shape[4]
    rhs = load_column.shape[0]
    inner = schur.shape[2]
    prims = coarse_basis.shape[2]
    owned, order = coarse_inverse.shape
    assert schur.shape[0] == 1 and schur.shape[1] == 1
    f32, bf16 = jnp.float32, jnp.bfloat16
    group = min(devices, 32)
    dma = pltpu.SemaphoreType.DMA
    hbm = pl.BlockSpec(memory_space=pl.ANY)
    result = pl.pallas_call(
        functools.partial(kernel, (subs, wides)),
        out_shape=pltpu.VMEM((4, rhs, width), f32),
        in_specs=[hbm] * 8,
        out_specs=pl.BlockSpec(memory_space=pltpu.VMEM),
        scratch_shapes=[
            pltpu.SMEM((4,), face_order.dtype),
            pltpu.SMEM((prims,), corner_map.dtype),
            pltpu.VMEM((patterns * 4, width), load_table.dtype),
            pltpu.VMEM((prims * 4, width), coarse_basis.dtype),
            pltpu.VMEM((owned, order), f32),
            pltpu.VMEM((1, rhs), load_column.dtype),
            pltpu.VMEM((4, 4, width, width), schur.dtype),
            pltpu.VMEM((4, 4, width, width), neumann.dtype),
            pltpu.VMEM((inner, inner), schur.dtype),
            pltpu.VMEM((inner, inner), neumann.dtype),
            pltpu.VMEM((4, patterns, width), f32),
            pltpu.VMEM((patterns, 4 * width), f32),
            pltpu.VMEM((2 * ITERS, 4, patterns, width), f32),
            pltpu.VMEM((2 * ITERS, 4, patterns, width), f32),
            pltpu.VMEM((4, 2 * prims, width), f32),
            pltpu.VMEM((4, 2 * prims, width), f32),
            pltpu.VMEM((wides, owned, order), f32),
            pltpu.VMEM((order, order), f32),
            pltpu.VMEM((5 * group * prims, MARK), f32),
            pltpu.VMEM((5 * prims, 4 * width), f32),
            pltpu.VMEM((5 * group * prims, order), bf16),
            pltpu.VMEM((rhs, 3 * patterns), bf16),
            pltpu.VMEM((2, order, 12 * width), bf16),
            pltpu.VMEM((4, order, width), f32),
            pltpu.VMEM((4, order, width), f32),
            pltpu.VMEM((ITERS, devices, prims, 5 * patterns + MARK), f32),
            pltpu.VMEM((group * prims, 5 * patterns), f32),
            pltpu.SemaphoreType.REGULAR,
            dma((6,)),
            dma((2, 4)),
            dma((2 * ITERS, 4)),
            dma((2 * ITERS, 4)),
            dma((4,)),
            dma((4,)),
            dma((4,)),
            dma((4,)),
            dma((wides,)),
            dma((wides,)),
            dma((ITERS,)),
            dma((ITERS,)),
        ],
        compiler_params=pltpu.CompilerParams(
            collective_id=0, has_side_effects=True, vmem_limit_bytes=VMEM_LIMIT
        ),
        name="bddc",
    )(
        face_order.reshape(4),
        corner_map.reshape(prims),
        load_table.reshape(patterns * 4, width),
        coarse_basis.reshape(prims * 4, width),
        coarse_inverse,
        load_column.reshape(1, rhs),
        schur.reshape(4, width, inner),
        neumann.reshape(4, width, inner),
    )
    return result.reshape(1, 1, 4, rhs, width)


def solution(mesh):
    in_specs = (
        P("sub", "wide", None, None, None),
        P(),
        P("sub", "wide", None),
        P("sub", "wide", None, None),
        P("sub", "wide", None, None),
        P("sub", "wide", None, None, None),
        P("sub", "wide", None),
        P("wide", None),
    )
    out_specs = P("sub", "wide", None, None, None)
    return jax.shard_map(body, mesh=mesh, in_specs=in_specs, out_specs=out_specs, check_vma=False)
```

```python
import functools

import jax
import jax.numpy as jnp
from jax import lax
from jax.experimental import pallas as pl
from jax.experimental.pallas import tpu as pltpu
from jax.sharding import PartitionSpec as P

ITERS = 3
damping = 0.3
MESH = pl.DeviceIdType.MESH
HIGHEST = lax.Precision.HIGHEST
OPPOSITE = (1, 0, 3, 2)
LANES = 128
VMEM_LIMIT = 56 * 1024 * 1024


def split(value):
    high = value.astype(jnp.bfloat16)
    low = (value - high.astype(jnp.float32)).astype(jnp.bfloat16)
    return high, low


def split3(value):
    high, low = split(value)
    rest = value - high.astype(jnp.float32) - low.astype(jnp.float32)
    return high, low, rest.astype(jnp.bfloat16)


def dot(a, b, dims=((1,), (0,)), precision=None):
    return lax.dot_general(
        a, b, (dims, ((), ())), precision=precision, preferred_element_type=jnp.float32
    )


def kernel(
    sizes,
    face_order_hbm,
    corner_map_hbm,
    load_table_hbm,
    basis_hbm,
    inverse_hbm,
    column_hbm,
    schur_hbm,
    neumann_hbm,
    out,
    face_order,
    corner_map,
    load_table,
    basis_in,
    inverse_in,
    column,
    schur_in,
    neumann_in,
    schur,
    neumann,
    load,
    sol,
    face_out,
    face_in,
    basis_out,
    basis_near,
    inverse_all,
    inverse_flat,
    gmat,
    hot,
    chosen,
    coarse,
    coarse_out,
    coarse_near,
    rest_all,
    wide_all,
    echo_all,
    far_sem,
    local_sem,
    block_sem,
    face_send,
    face_recv,
    basis_send,
    basis_recv,
    coarse_send,
    coarse_recv,
    inverse_send,
    inverse_recv,
    rest_send,
    rest_recv,
):
    subs, wides = sizes
    devices = subs * wides
    rhs, width = load.shape[1], load.shape[2]
    inner = 4 * width
    prims = basis_out.shape[1] // 2
    order = inverse_flat.shape[0]
    owned = inverse_in.shape[0]
    group = min(devices, 32)
    marked = prims * rhs
    small_mesh = devices <= 32
    row = lax.axis_index("sub")
    col = lax.axis_index("wide")
    me = row * wides + col
    has = (row > 0, row < subs - 1, col > 0, col < wides - 1)
    near = ((row - 1, col), (row + 1, col), (row, col - 1), (row, col + 1))
    share = [jnp.where(flag, jnp.float32(0.5), jnp.float32(1.0)) for flag in has]
    faces = range(4)

    pairs = (
        (load_table_hbm, load_table),
        (basis_hbm, basis_in),
        (corner_map_hbm, corner_map),
        (face_order_hbm, face_order),
        (inverse_hbm, inverse_in),
        (column_hbm, column),
    )
    fetch = [
        pltpu.make_async_copy(source, target, local_sem.at[i])
        for i, (source, target) in enumerate(pairs)
    ]
    blocks = [
        [
            pltpu.make_async_copy(
                source.at[:, :, b * width : (b + 1) * width], target.at[b], sems.at[b]
            )
            for b in faces
        ]
        for source, target, sems in (
            (neumann_hbm, neumann_in, block_sem.at[0]),
            (schur_hbm, schur_in, block_sem.at[1]),
        )
    ]
    for copy in fetch[:3]:
        copy.start()

    def loop(first, last, action):
        if small_mesh:
            for step in range(first, last):
                action(step)
        else:

            def one(step, carry):
                action(step)
                return carry

            lax.fori_loop(first, last, one, 0)

    def each_wide(action):
        loop(1, wides, lambda step: action(lax.rem(col + step, wides)))

    def each_sub(action):
        loop(1, subs, lambda step: action(lax.rem(row + step, subs)))

    barrier = pltpu.get_barrier_semaphore()

    def signal(sem, where):
        pl.semaphore_signal(sem, inc=1, device_id=where, device_id_type=MESH)

    each_sub(lambda other: signal(barrier, (other, col)))
    each_wide(lambda other: signal(barrier, (row, other)))
    for copy in fetch[3:] + blocks[0] + blocks[1]:
        copy.start()

    def face_copy(turn, f):
        return pltpu.make_async_remote_copy(
            src_ref=face_out.at[turn, f],
            dst_ref=face_in.at[turn, OPPOSITE[f]],
            send_sem=face_send.at[turn, f],
            recv_sem=face_recv.at[turn, OPPOSITE[f]],
            device_id=near[f],
            device_id_type=MESH,
        )

    def to_near(source, target, send, recv, f):
        return pltpu.make_async_remote_copy(
            src_ref=source.at[f],
            dst_ref=target.at[OPPOSITE[f]],
            send_sem=send.at[f],
            recv_sem=recv.at[OPPOSITE[f]],
            device_id=near[f],
            device_id_type=MESH,
        )

    def basis_copy(f):
        return to_near(basis_out, basis_near, basis_send, basis_recv, f)

    def coarse_copy(f):
        return to_near(coarse_out, coarse_near, coarse_send, coarse_recv, f)

    def inverse_copy(other):
        return pltpu.make_async_remote_copy(
            src_ref=inverse_all.at[col],
            dst_ref=inverse_all.at[col],
            send_sem=inverse_send.at[other],
            recv_sem=inverse_recv.at[col],
            device_id=(row, other),
            device_id_type=MESH,
        )

    def spread_copy(blocks, sems, where):
        return pltpu.make_async_remote_copy(
            src_ref=blocks.at[me],
            dst_ref=blocks.at[me],
            send_sem=sems[0],
            recv_sem=sems[1],
            device_id=where,
            device_id_type=MESH,
        )

    def sems_of(i):
        return rest_send.at[i], rest_recv.at[i]

    def each_near(action):
        for f in faces:

            @pl.when(has[f])
            def _():
                action(f)

    def wait_near(target, recv):
        each_near(lambda f: pltpu.make_async_copy(target.at[f], target.at[f], recv.at[f]).wait())

    def wait_others(blocks, sem):
        others = blocks.at[pl.ds(0, devices - 1)]
        pltpu.make_async_copy(others, others, sem).wait()

    def send_faces(turn):
        each_near(lambda f: face_copy(turn, f).start())

    def wait_faces(turn):
        wait_near(face_in.at[turn], face_recv.at[turn])

    def drain_faces(turn):
        each_near(lambda f: face_copy(turn, f).wait_send())

    upper = row < (subs + 1) // 2
    half = subs // 2

    def send_all(blocks, sems):
        def rows(i):
            there = jnp.where(upper, subs - 1 - i, i)

            def columns(step):
                other = lax.rem(col + step, wides)

                def start():
                    spread_copy(blocks, sems, (there, other)).start()

                if isinstance(step, int) and (step > 0 or i < half):
                    start()
                else:
                    pl.when(jnp.logical_or(there != row, step != 0))(start)

            loop(0, wides, columns)

        loop(0, subs, rows)

    def side(values):
        return jnp.concatenate(values, axis=1)

    def cut(value):
        return [value[:, f * width : (f + 1) * width] for f in faces]

    def arranged(rows):
        target = 4 * lax.broadcasted_iota(jnp.int32, (rows, 4 * rows), 0)
        source = lax.broadcasted_iota(jnp.int32, (rows, 4 * rows), 1)
        picks = [(source == target + f).astype(jnp.float32) for f in faces]
        return jnp.concatenate(picks, axis=0).astype(jnp.bfloat16)

    table_picks = arranged(rhs)
    basis_picks = arranged(prims)
    weights = side([share[f] * jnp.ones((1, width), jnp.float32) for f in faces])

    fetch[0].wait()
    table = dot(table_picks, load_table[...])
    for f in faces:
        load[f] = table[f * rhs : (f + 1) * rhs]
        face_out[0, f] = table[f * rhs : (f + 1) * rhs]
    fetch[1].wait()
    fetch[2].wait()
    own = dot(basis_picks, basis_in[...])
    row_of = lax.broadcasted_iota(jnp.int32, (prims, width), 0)
    marks = jnp.zeros((prims, width), jnp.int32)
    for p in range(prims):
        marks = jnp.where(row_of == p, corner_map[p], marks)
    marks = marks.astype(jnp.float32)
    lane_of = lax.broadcasted_iota(jnp.int32, (1, LANES - marked), 1)
    mark_row = jnp.zeros((1, LANES - marked), jnp.int32)
    for p in range(prims):
        mark_row = jnp.where(lane_of == p, corner_map[p], mark_row)
    mark_row = mark_row.astype(jnp.float32)
    own_basis = side([own[f * prims : (f + 1) * prims] for f in faces]).astype(jnp.bfloat16)
    for f in faces:
        basis_out[f] = jnp.concatenate([own[f * prims : (f + 1) * prims], marks], axis=0)

    pl.semaphore_wait(barrier, subs - 1 + wides - 1)
    send_faces(0)
    each_near(lambda f: basis_copy(f).start())
    each_wide(lambda other: signal(far_sem, (row, other)))
    fetch[4].wait()
    inverse_all[col] = inverse_in[...]
    each_wide(lambda other: inverse_copy(other).start())

    for f in faces:

        @pl.when(jnp.logical_not(has[f]))
        def _():
            for turn in range(2 * ITERS):
                face_in[turn, f] = jnp.zeros((rhs, width), jnp.float32)
            basis_near[f] = jnp.zeros(basis_near.shape[1:], jnp.float32)
            coarse_near[f] = jnp.zeros(coarse_near.shape[1:], jnp.float32)

    fetch[3].wait()
    spot = []
    for f in faces:
        found = jnp.int32(0)
        for b in range(1, 4):
            found = jnp.where(face_order[b] == f, jnp.int32(b), found)
        spot.append(found)

    def by_face(source, target):
        for f in faces:
            for g in faces:
                target[f * width : (f + 1) * width, g * width : (g + 1) * width] = source[
                    spot[g], spot[f]
                ]

    for copy in blocks[0]:
        copy.wait()
    by_face(neumann_in, neumann)

    def weighted(turn):
        return side([share[f] * (face_out[turn, f] + face_in[turn, f]) for f in faces])

    def apply_neumann(turn, values):
        result = dot(values.astype(jnp.bfloat16), neumann[...])
        for f, part in enumerate(cut(result)):
            face_out[turn, f] = part
        send_faces(turn)

    def by_pattern(left, values):
        high, low = split(values)
        both = dot(left, jnp.concatenate([high, low], axis=0), ((1,), (1,)))
        return both[:, : values.shape[0]] + both[:, values.shape[0] :]

    def restrict(iteration, values):
        parts = by_pattern(own_basis, values)
        rest_all[iteration, me] = side([parts[p : p + 1] for p in range(prims)] + [mark_row])

    wait_faces(0)
    residual = weighted(0)
    apply_neumann(1, residual)
    restrict(0, residual)
    pl.semaphore_wait(far_sem, wides - 1)
    send_all(rest_all.at[0], sems_of(0))

    wait_near(basis_near, basis_recv)
    gmat[...] = jnp.zeros(gmat.shape, jnp.float32)
    gmat[0:prims, :] = side([basis_out[f, :prims] for f in faces])
    for f in faces:
        gmat[(f + 1) * prims : (f + 2) * prims, f * width : (f + 1) * width] = basis_near[
            f, :prims
        ]
    shared = (gmat[...] * weights).astype(jnp.bfloat16)

    for copy in blocks[1]:
        copy.wait()
    by_face(schur_in, schur)
    each_wide(
        lambda other: pltpu.make_async_copy(
            inverse_all.at[other], inverse_all.at[other], inverse_recv.at[other]
        ).wait()
    )
    for w in range(wides):
        inverse_flat[w * owned : (w + 1) * owned, :] = inverse_all[w]
    lanes = lax.broadcasted_iota(jnp.int32, (prims, order), 1).astype(jnp.float32)
    picks = [marks[:, :1] == lanes]
    picks += [basis_near[f, prims:, :1] == lanes for f in faces]
    mine = jnp.concatenate([flag.astype(jnp.float32) for flag in picks], axis=0)
    dense = dot(mine.T.astype(jnp.bfloat16), gmat[...].astype(jnp.bfloat16))
    spread = damping * weights * dot(inverse_flat[...], dense, ((1,), (0,)), HIGHEST)
    high, low = split(spread)
    coarse[0, :, :inner], coarse[1, :, :inner] = high, low
    both = dot(jnp.concatenate([high, low], axis=0), schur[...])
    effect = both[:order] + both[order:]
    for f, part in enumerate(cut(effect)):
        coarse_out[f] = part
    each_near(lambda f: coarse_copy(f).start())

    def apply_schur(turn, values):
        high, low = split(values)
        both = dot(jnp.concatenate([high, low], axis=0), schur[...])
        for f, part in enumerate(cut(both[:rhs] + both[rhs:])):
            face_out[turn, f] = load[f] - part
        send_faces(turn)

    def hot_of(part):
        numbers = rest_all[0, pl.ds(part * group, group), 0, :]
        lanes = lax.broadcasted_iota(jnp.int32, (group, order), 1).astype(jnp.float32)
        return numbers, [
            numbers[:, marked + p : marked + p + 1] == lanes for p in range(prims)
        ]

    def joined_hot(flags):
        return jnp.concatenate([flag.astype(jnp.float32) for flag in flags], axis=0).astype(
            jnp.bfloat16
        )

    def mark():
        numbers, flags = hot_of(0)
        for shift in (-wides, wides, -1, 1):
            cutoff = shift % devices
            moved = jnp.concatenate([numbers[cutoff:], numbers[:cutoff]], axis=0)
            lanes = lax.broadcasted_iota(jnp.int32, (group, order), 1).astype(jnp.float32)
            flags = flags + [
                moved[:, marked + p : marked + p + 1] == lanes for p in range(prims)
            ]
        hot[...] = joined_hot(flags)

    def total_of(rows, high_hot):
        high, low = split(rows)
        both = dot(jnp.concatenate([high, low], axis=0), high_hot)
        return both[: rows.shape[0]] + both[rows.shape[0] :]

    def gather(iteration):
        def one(part, own_hot):
            turned = rest_all[iteration, pl.ds(part * group, group), 0, :].T
            return total_of(side([turned[p * rhs : (p + 1) * rhs] for p in range(prims)]), own_hot)

        wait_others(rest_all.at[iteration], rest_recv.at[iteration])
        if small_mesh:
            if iteration == 0:
                mark()
            return one(0, hot[: prims * group])
        return lax.fori_loop(
            0,
            devices // group,
            lambda part, total: total + one(part, joined_hot(hot_of(part)[1])),
            jnp.zeros((rhs, order), jnp.float32),
        )

    def send_echo(values):
        parts = by_pattern(own_basis, values)
        blank = jnp.zeros((1, LANES - 2 * order), jnp.float32)
        rows = [side([parts[p : p + 1], parts[p + 1 : p + 2], blank]) for p in range(0, prims, 2)]
        echo_all[me] = jnp.concatenate(rows, axis=0)
        send_all(echo_all, sems_of(ITERS))

    def gather_echo():
        wait_others(echo_all, rest_recv.at[ITERS])
        turned = [echo_all[:, i, :].T for i in range(prims // 2)]
        pieces = [
            turned[p // 2][p % 2 * order : (p % 2 + 1) * order] for p in range(prims)
        ]
        return total_of(side(pieces), hot[: prims * group])

    chunks = LANES // rhs
    wide_rows = -(-5 * prims // chunks)

    def send_wide(values):
        parts = by_pattern(shared, values)
        pieces = [parts[i : i + 1] for i in range(5 * prims)]
        pieces += [jnp.zeros((1, rhs), jnp.float32)] * (wide_rows * chunks - 5 * prims)
        rows = [side(pieces[i * chunks : (i + 1) * chunks]) for i in range(wide_rows)]
        wide_all[me] = jnp.concatenate(rows, axis=0)
        send_all(wide_all, sems_of(ITERS - 1))

    def gather_wide():
        wait_others(wide_all, rest_recv.at[ITERS - 1])
        turned = [wide_all[:, i, :].T for i in range(wide_rows)]
        pieces = [
            turned[i // chunks][i % chunks * rhs : (i % chunks + 1) * rhs]
            for i in range(5 * prims)
        ]
        return total_of(side(pieces), hot[...])

    def correct(total, columns):
        high, low = split(total)
        both = dot(jnp.concatenate([high, low], axis=0), coarse[0, :, :columns])
        return both[:rhs] + both[rhs:] + dot(high, coarse[1, :, :columns])

    def expand(values):
        return dot(chosen[...], jnp.concatenate(split3(values), axis=0))

    scaled = damping * weights

    def advanced(turn, base):
        change = scaled * side([face_out[turn, f] + face_in[turn, f] for f in faces])
        return change if base is None else base + change

    drain_faces(0)
    each_near(lambda f: basis_copy(f).wait_send())
    wait_faces(1)
    sol[...] = advanced(1, None)

    for iteration in range(1, ITERS):
        first = 2 * iteration
        last = iteration == ITERS - 1
        apply_schur(first, sol[...])
        if iteration == 1:
            wait_near(coarse_near, coarse_recv)
            joined = [coarse_out[f] + coarse_near[f] for f in faces]
            effect = weights * side(joined)
            high, low = split(effect)
            coarse[0, :, inner:], coarse[1, :, inner:] = high, low
            if small_mesh:
                send_echo(effect)
            fetch[5].wait()
            wanted = lax.broadcasted_iota(jnp.int32, (rhs, column.shape[1]), 0) == column[...]
            wanted = wanted.astype(jnp.float32).T.astype(jnp.bfloat16)
            chosen[...] = side([wanted, wanted, wanted])
        if last and small_mesh:
            send_wide(side([face_out[first, f] for f in faces]))
        total = gather(iteration - 1)
        change = correct(total, 2 * inner)
        sol[...] += change[:, :inner]
        wait_faces(first)
        residual = weighted(first) - change[:, inner:]
        apply_neumann(first + 1, residual)
        if not (last and small_mesh):
            restrict(iteration, residual)
            send_all(rest_all.at[iteration], sems_of(iteration))
        drain_faces(first - 1)
        drain_faces(first)
        if last:
            if small_mesh:
                high, low = split(total)
                echo_high, echo_low = split(gather_echo())
                both = dot(jnp.concatenate([high, low], axis=0), echo_high)
                total = gather_wide() - (both[:rhs] + both[rhs:] + dot(high, echo_low))
            else:
                total = gather(iteration)
            change = correct(total, inner)
            for f, part in enumerate(cut(expand(sol[...] + change))):
                out[f] = part
            wait_faces(first + 1)
            for f, part in enumerate(cut(expand(advanced(first + 1, None)))):
                out[f] = out[f] + part
        else:
            wait_faces(first + 1)
            sol[...] = advanced(first + 1, sol[...])

    drain_faces(2 * ITERS - 1)
    each_near(lambda f: coarse_copy(f).wait_send())
    each_wide(lambda other: inverse_copy(other).wait_send())
    for iteration in range(ITERS - 1 if small_mesh else ITERS):
        wait_others(rest_all.at[iteration], rest_send.at[iteration])
    if small_mesh:
        wait_others(wide_all, rest_send.at[ITERS - 1])
        wait_others(echo_all, rest_send.at[ITERS])


def body(
    load_table, load_column, face_order, schur, neumann, coarse_basis, corner_map, coarse_inverse
):
    subs, wides = lax.axis_size("sub"), lax.axis_size("wide")
    devices = subs * wides
    patterns, width = load_table.shape[2], load_table.shape[4]
    rhs = load_column.shape[0]
    inner = schur.shape[2]
    prims = coarse_basis.shape[2]
    owned, order = coarse_inverse.shape
    assert schur.shape[0] == 1 and schur.shape[1] == 1
    f32, bf16 = jnp.float32, jnp.bfloat16
    group = min(devices, 32)
    dma = pltpu.SemaphoreType.DMA
    hbm = pl.BlockSpec(memory_space=pl.ANY)
    result = pl.pallas_call(
        functools.partial(kernel, (subs, wides)),
        out_shape=pltpu.VMEM((4, rhs, width), f32),
        in_specs=[hbm] * 8,
        out_specs=pl.BlockSpec(memory_space=pltpu.VMEM),
        scratch_shapes=[
            pltpu.SMEM((4,), face_order.dtype),
            pltpu.SMEM((prims,), corner_map.dtype),
            pltpu.VMEM((patterns * 4, width), load_table.dtype),
            pltpu.VMEM((prims * 4, width), coarse_basis.dtype),
            pltpu.VMEM((owned, order), f32),
            pltpu.VMEM((1, rhs), load_column.dtype),
            pltpu.VMEM((4, 4, width, width), schur.dtype),
            pltpu.VMEM((4, 4, width, width), neumann.dtype),
            pltpu.VMEM((inner, inner), schur.dtype),
            pltpu.VMEM((inner, inner), neumann.dtype),
            pltpu.VMEM((4, patterns, width), f32),
            pltpu.VMEM((patterns, 4 * width), f32),
            pltpu.VMEM((2 * ITERS, 4, patterns, width), f32),
            pltpu.VMEM((2 * ITERS, 4, patterns, width), f32),
            pltpu.VMEM((4, 2 * prims, width), f32),
            pltpu.VMEM((4, 2 * prims, width), f32),
            pltpu.VMEM((wides, owned, order), f32),
            pltpu.VMEM((order, order), f32),
            pltpu.VMEM((5 * prims, 4 * width), f32),
            pltpu.VMEM((5 * group * prims, order if devices == group else LANES), bf16),
            pltpu.VMEM((rhs, 3 * patterns), bf16),
            pltpu.VMEM((2, order, 8 * width), bf16),
            pltpu.VMEM((4, order, width), f32),
            pltpu.VMEM((4, order, width), f32),
            pltpu.VMEM((ITERS, devices, 1, LANES), f32),
            pltpu.VMEM((group, -(-5 * prims * patterns // LANES), LANES), f32),
            pltpu.VMEM((group, prims // 2, LANES), f32),
            pltpu.SemaphoreType.REGULAR,
            dma((6,)),
            dma((2, 4)),
            dma((2 * ITERS, 4)),
            dma((2 * ITERS, 4)),
            dma((4,)),
            dma((4,)),
            dma((4,)),
            dma((4,)),
            dma((wides,)),
            dma((wides,)),
            dma((ITERS + 1,)),
            dma((ITERS + 1,)),
        ],
        compiler_params=pltpu.CompilerParams(
            collective_id=0, has_side_effects=True, vmem_limit_bytes=VMEM_LIMIT
        ),
        name="bddc",
    )(
        face_order.reshape(4),
        corner_map.reshape(prims),
        load_table.reshape(patterns * 4, width),
        coarse_basis.reshape(prims * 4, width),
        coarse_inverse,
        load_column.reshape(1, rhs),
        schur.reshape(4, width, inner),
        neumann.reshape(4, width, inner),
    )
    return result.reshape(1, 1, 4, rhs, width)


def solution(mesh):
    in_specs = (
        P("sub", "wide", None, None, None),
        P(),
        P("sub", "wide", None),
        P("sub", "wide", None, None),
        P("sub", "wide", None, None),
        P("sub", "wide", None, None, None),
        P("sub", "wide", None),
        P("wide", None),
    )
    out_specs = P("sub", "wide", None, None, None)
    return jax.shard_map(body, mesh=mesh, in_specs=in_specs, out_specs=out_specs, check_vma=False)
```

```python
import functools

import jax
import jax.numpy as jnp
from jax import lax
from jax.experimental import pallas as pl
from jax.experimental.pallas import tpu as pltpu
from jax.sharding import PartitionSpec as P

ITERS = 3
damping = 0.3
MESH = pl.DeviceIdType.MESH
HIGHEST = lax.Precision.HIGHEST
OPPOSITE = (1, 0, 3, 2)
LANES = 128
VMEM_LIMIT = 56 * 1024 * 1024


def split(value):
    high = value.astype(jnp.bfloat16)
    low = (value - high.astype(jnp.float32)).astype(jnp.bfloat16)
    return high, low


def split3(value):
    high, low = split(value)
    rest = value - high.astype(jnp.float32) - low.astype(jnp.float32)
    return high, low, rest.astype(jnp.bfloat16)


def dot(a, b, dims=((1,), (0,)), precision=None):
    return lax.dot_general(
        a, b, (dims, ((), ())), precision=precision, preferred_element_type=jnp.float32
    )


def kernel(
    sizes,
    face_order_hbm,
    corner_map_hbm,
    load_table_hbm,
    basis_hbm,
    inverse_hbm,
    column_hbm,
    schur_hbm,
    neumann_hbm,
    out,
    face_order,
    corner_map,
    load_table,
    basis_in,
    inverse_in,
    column,
    schur_in,
    neumann_in,
    schur,
    neumann,
    load,
    sol,
    face_out,
    face_in,
    basis_out,
    basis_near,
    inverse_all,
    inverse_flat,
    spread_out,
    gmat,
    hot,
    chosen,
    coarse,
    coarse_out,
    coarse_near,
    first,
    second_out,
    second_near,
    rest_all,
    wide_all,
    echo_all,
    far_sem,
    local_sem,
    block_sem,
    face_send,
    face_recv,
    basis_send,
    basis_recv,
    coarse_send,
    coarse_recv,
    second_send,
    second_recv,
    inverse_send,
    inverse_recv,
    rest_send,
    rest_recv,
):
    subs, wides = sizes
    devices = subs * wides
    rhs, width = load.shape[1], load.shape[2]
    inner = 4 * width
    prims = basis_out.shape[1] // 2
    order = inverse_flat.shape[0]
    owned = inverse_in.shape[0]
    group = min(devices, 32)
    marked = prims * rhs
    small_mesh = devices <= 32
    row = lax.axis_index("sub")
    col = lax.axis_index("wide")
    me = row * wides + col
    has = (row > 0, row < subs - 1, col > 0, col < wides - 1)
    near = ((row - 1, col), (row + 1, col), (row, col - 1), (row, col + 1))
    share = [jnp.where(flag, jnp.float32(0.5), jnp.float32(1.0)) for flag in has]
    faces = range(4)

    pairs = (
        (load_table_hbm, load_table),
        (basis_hbm, basis_in),
        (corner_map_hbm, corner_map),
        (face_order_hbm, face_order),
        (inverse_hbm, inverse_in),
        (column_hbm, column),
    )
    fetch = [
        pltpu.make_async_copy(source, target, local_sem.at[i])
        for i, (source, target) in enumerate(pairs)
    ]
    blocks = [
        [
            pltpu.make_async_copy(
                source.at[:, :, b * width : (b + 1) * width], target.at[b], sems.at[b]
            )
            for b in faces
        ]
        for source, target, sems in (
            (neumann_hbm, neumann_in, block_sem.at[0]),
            (schur_hbm, schur_in, block_sem.at[1]),
        )
    ]
    for copy in fetch[:3]:
        copy.start()

    def loop(first, last, action):
        if small_mesh:
            for step in range(first, last):
                action(step)
        else:

            def one(step, carry):
                action(step)
                return carry

            lax.fori_loop(first, last, one, 0)

    def each_wide(action):
        loop(1, wides, lambda step: action(lax.rem(col + step, wides)))

    def each_sub(action):
        loop(1, subs, lambda step: action(lax.rem(row + step, subs)))

    barrier = pltpu.get_barrier_semaphore()

    def signal(sem, where):
        pl.semaphore_signal(sem, inc=1, device_id=where, device_id_type=MESH)

    stepwise = subs <= 4 and wides <= 8
    near_by = [(-1, 0), (1, 0), (0, -1), (0, 1), (0, -3), (0, 3)]
    around = {(a + c, b + d) for a, b in near_by for c, d in near_by} | set(near_by)
    around = sorted(around - {(0, 0)})

    def present(steps):
        return [
            (
                jnp.logical_and(
                    jnp.logical_and(row + r >= 0, row + r < subs),
                    jnp.logical_and(col + c >= 0, col + c < wides),
                ),
                (row + r, col + c),
            )
            for r, c in steps
        ]

    known, known_twice = present(near_by), present(around)
    if stepwise:
        greeted = sum(flag.astype(jnp.int32) for flag, _ in known)
        greeted_twice = sum(flag.astype(jnp.int32) for flag, _ in known_twice)
    else:
        greeted = subs - 1 + wides - 1

    def greet(sem, those=known):
        for flag, where in those:

            @pl.when(flag)
            def _():
                signal(sem, where)

    if stepwise:
        greet(barrier)
    else:
        each_sub(lambda other: signal(barrier, (other, col)))
        each_wide(lambda other: signal(barrier, (row, other)))
    for copy in fetch[3:] + blocks[0] + blocks[1]:
        copy.start()

    def face_copy(turn, f):
        return pltpu.make_async_remote_copy(
            src_ref=face_out.at[turn, f],
            dst_ref=face_in.at[turn, OPPOSITE[f]],
            send_sem=face_send.at[turn, f],
            recv_sem=face_recv.at[turn, OPPOSITE[f]],
            device_id=near[f],
            device_id_type=MESH,
        )

    def to_near(source, target, send, recv, f):
        return pltpu.make_async_remote_copy(
            src_ref=source.at[f],
            dst_ref=target.at[OPPOSITE[f]],
            send_sem=send.at[f],
            recv_sem=recv.at[OPPOSITE[f]],
            device_id=near[f],
            device_id_type=MESH,
        )

    def basis_copy(f):
        return to_near(basis_out, basis_near, basis_send, basis_recv, f)

    def coarse_copy(f):
        return to_near(coarse_out, coarse_near, coarse_send, coarse_recv, f)

    def second_copy(f):
        return to_near(second_out, second_near, second_send, second_recv, f)

    def inverse_copy(other):
        return pltpu.make_async_remote_copy(
            src_ref=inverse_all.at[col],
            dst_ref=inverse_all.at[col],
            send_sem=inverse_send.at[other],
            recv_sem=inverse_recv.at[col],
            device_id=(row, other),
            device_id_type=MESH,
        )

    def spread_copy(blocks, sems, where):
        return pltpu.make_async_remote_copy(
            src_ref=blocks.at[me],
            dst_ref=blocks.at[me],
            send_sem=sems[0],
            recv_sem=sems[1],
            device_id=where,
            device_id_type=MESH,
        )

    def sems_of(i):
        return rest_send.at[i], rest_recv.at[i]

    def each_near(action):
        for f in faces:

            @pl.when(has[f])
            def _():
                action(f)

    def wait_near(target, recv):
        each_near(lambda f: pltpu.make_async_copy(target.at[f], target.at[f], recv.at[f]).wait())

    def wait_others(blocks, sem):
        others = blocks.at[pl.ds(0, devices - 1)]
        pltpu.make_async_copy(others, others, sem).wait()

    def send_faces(turn):
        each_near(lambda f: face_copy(turn, f).start())

    def wait_faces(turn):
        wait_near(face_in.at[turn], face_recv.at[turn])

    def drain_faces(turn):
        each_near(lambda f: face_copy(turn, f).wait_send())

    upper = row < (subs + 1) // 2
    half = subs // 2

    def send_all(blocks, sems):
        def rows(i):
            there = jnp.where(upper, subs - 1 - i, i)

            def columns(step):
                other = lax.rem(col + step, wides)

                def start():
                    spread_copy(blocks, sems, (there, other)).start()

                if isinstance(step, int) and (step > 0 or i < half):
                    start()
                else:
                    pl.when(jnp.logical_or(there != row, step != 0))(start)

            loop(0, wides, columns)

        loop(0, subs, rows)

    def side(values):
        return jnp.concatenate(values, axis=1)

    def cut(value):
        return [value[:, f * width : (f + 1) * width] for f in faces]

    def arranged(rows):
        target = 4 * lax.broadcasted_iota(jnp.int32, (rows, 4 * rows), 0)
        source = lax.broadcasted_iota(jnp.int32, (rows, 4 * rows), 1)
        picks = [(source == target + f).astype(jnp.float32) for f in faces]
        return jnp.concatenate(picks, axis=0).astype(jnp.bfloat16)

    table_picks = arranged(rhs)
    basis_picks = arranged(prims)
    weights = side([share[f] * jnp.ones((1, width), jnp.float32) for f in faces])

    fetch[0].wait()
    table = dot(table_picks, load_table[...])
    for f in faces:
        load[f] = table[f * rhs : (f + 1) * rhs]
        face_out[0, f] = table[f * rhs : (f + 1) * rhs]
    pl.semaphore_wait(barrier, greeted)
    send_faces(0)
    if stepwise:
        greet(far_sem.at[0])
    else:
        each_wide(lambda other: signal(far_sem.at[1], (row, other)))
    fetch[1].wait()
    fetch[2].wait()
    own = dot(basis_picks, basis_in[...])
    row_of = lax.broadcasted_iota(jnp.int32, (prims, width), 0)
    marks = jnp.zeros((prims, width), jnp.int32)
    for p in range(prims):
        marks = jnp.where(row_of == p, corner_map[p], marks)
    marks = marks.astype(jnp.float32)
    lane_of = lax.broadcasted_iota(jnp.int32, (1, LANES - marked), 1)
    mark_row = jnp.zeros((1, LANES - marked), jnp.int32)
    for p in range(prims):
        mark_row = jnp.where(lane_of == p, corner_map[p], mark_row)
    mark_row = mark_row.astype(jnp.float32)
    own_basis = side([own[f * prims : (f + 1) * prims] for f in faces]).astype(jnp.bfloat16)
    for f in faces:
        basis_out[f] = jnp.concatenate([own[f * prims : (f + 1) * prims], marks], axis=0)

    each_near(lambda f: basis_copy(f).start())

    for f in faces:

        @pl.when(jnp.logical_not(has[f]))
        def _():
            for turn in range(2 * ITERS):
                face_in[turn, f] = jnp.zeros((rhs, width), jnp.float32)
            basis_near[f] = jnp.zeros(basis_near.shape[1:], jnp.float32)
            coarse_near[f] = jnp.zeros(coarse_near.shape[1:], jnp.float32)
            second_near[f] = jnp.zeros(second_near.shape[1:], jnp.float32)

    fetch[3].wait()
    spot = []
    for f in faces:
        found = jnp.int32(0)
        for b in range(1, 4):
            found = jnp.where(face_order[b] == f, jnp.int32(b), found)
        spot.append(found)

    def by_face(source, target):
        for f in faces:
            for g in faces:
                target[f * width : (f + 1) * width, g * width : (g + 1) * width] = source[
                    spot[g], spot[f]
                ]

    for copy in blocks[0]:
        copy.wait()
    by_face(neumann_in, neumann)

    def weighted(turn):
        return side([share[f] * (face_out[turn, f] + face_in[turn, f]) for f in faces])

    def apply_neumann(turn, values):
        result = dot(values.astype(jnp.bfloat16), neumann[...])
        for f, part in enumerate(cut(result)):
            face_out[turn, f] = part
        send_faces(turn)

    def by_pattern(left, values):
        high, low = split(values)
        both = dot(left, jnp.concatenate([high, low], axis=0), ((1,), (1,)))
        return both[:, : values.shape[0]] + both[:, values.shape[0] :]

    def restrict(iteration, values):
        parts = by_pattern(own_basis, values)
        rest_all[iteration, me] = side([parts[p : p + 1] for p in range(prims)] + [mark_row])

    fetch[4].wait()
    inverse_all[col] = inverse_in[...]
    if stepwise:
        pl.semaphore_wait(far_sem.at[0], greeted)
        greet(far_sem.at[1], known_twice)
    wait_faces(0)
    residual = weighted(0)
    apply_neumann(1, residual)
    restrict(0, residual)
    if stepwise:
        pl.semaphore_wait(far_sem.at[1], greeted_twice)
        greet(far_sem.at[2], known_twice)

    wait_near(basis_near, basis_recv)
    gmat[...] = jnp.zeros(gmat.shape, jnp.float32)
    gmat[0:prims, :] = side([basis_out[f, :prims] for f in faces])
    for f in faces:
        gmat[(f + 1) * prims : (f + 2) * prims, f * width : (f + 1) * width] = basis_near[
            f, :prims
        ]
    shared = (gmat[...] * weights).astype(jnp.bfloat16)

    for copy in blocks[1]:
        copy.wait()
    by_face(schur_in, schur)
    lanes = lax.broadcasted_iota(jnp.int32, (prims, order), 1).astype(jnp.float32)
    picks = [marks[:, :1] == lanes]
    picks += [basis_near[f, prims:, :1] == lanes for f in faces]
    mine = jnp.concatenate([flag.astype(jnp.float32) for flag in picks], axis=0)
    dense = dot(mine.T.astype(jnp.bfloat16), gmat[...].astype(jnp.bfloat16))
    spread_out[...] = damping * weights * dense
    high, low = split(spread_out[...])
    both = dot(jnp.concatenate([high, low], axis=0), schur[...])
    effect = both[:order] + both[order:]
    for f, part in enumerate(cut(effect)):
        coarse_out[f] = part
    each_near(lambda f: coarse_copy(f).start())
    if stepwise:
        pl.semaphore_wait(far_sem.at[2], greeted_twice)
    else:
        pl.semaphore_wait(far_sem.at[1], wides - 1)
    send_all(rest_all.at[0], sems_of(0))
    each_wide(lambda other: inverse_copy(other).start())

    def apply_schur(turn, values):
        high, low = split(values)
        both = dot(jnp.concatenate([high, low], axis=0), schur[...])
        for f, part in enumerate(cut(both[:rhs] + both[rhs:])):
            face_out[turn, f] = load[f] - part
        send_faces(turn)

    def hot_of(part):
        numbers = rest_all[0, pl.ds(part * group, group), 0, :]
        lanes = lax.broadcasted_iota(jnp.int32, (group, order), 1).astype(jnp.float32)
        return numbers, [
            numbers[:, marked + p : marked + p + 1] == lanes for p in range(prims)
        ]

    def joined_hot(flags):
        return jnp.concatenate([flag.astype(jnp.float32) for flag in flags], axis=0).astype(
            jnp.bfloat16
        )

    def mark():
        numbers, flags = hot_of(0)
        for shift in (-wides, wides, -1, 1):
            cutoff = shift % devices
            moved = jnp.concatenate([numbers[cutoff:], numbers[:cutoff]], axis=0)
            lanes = lax.broadcasted_iota(jnp.int32, (group, order), 1).astype(jnp.float32)
            flags = flags + [
                moved[:, marked + p : marked + p + 1] == lanes for p in range(prims)
            ]
        hot[...] = joined_hot(flags)

    def total_of(rows, high_hot):
        high, low = split(rows)
        both = dot(jnp.concatenate([high, low], axis=0), high_hot)
        return both[: rows.shape[0]] + both[rows.shape[0] :]

    def gather(iteration):
        def one(part, own_hot):
            turned = rest_all[iteration, pl.ds(part * group, group), 0, :].T
            return total_of(side([turned[p * rhs : (p + 1) * rhs] for p in range(prims)]), own_hot)

        wait_others(rest_all.at[iteration], rest_recv.at[iteration])
        if small_mesh:
            if iteration == 0:
                mark()
            return one(0, hot[: prims * group])
        return lax.fori_loop(
            0,
            devices // group,
            lambda part, total: total + one(part, joined_hot(hot_of(part)[1])),
            jnp.zeros((rhs, order), jnp.float32),
        )

    def send_echo(values):
        parts = by_pattern(own_basis, values)
        blank = jnp.zeros((1, LANES - 2 * order), jnp.float32)
        rows = [side([parts[p : p + 1], parts[p + 1 : p + 2], blank]) for p in range(0, prims, 2)]
        echo_all[me] = jnp.concatenate(rows, axis=0)
        send_all(echo_all, sems_of(ITERS))

    def gather_echo():
        wait_others(echo_all, rest_recv.at[ITERS])
        turned = [echo_all[:, i, :].T for i in range(prims // 2)]
        pieces = [
            turned[p // 2][p % 2 * order : (p % 2 + 1) * order] for p in range(prims)
        ]
        return total_of(side(pieces), hot[: prims * group])

    chunks = LANES // rhs
    wide_rows = -(-5 * prims // chunks)

    def send_wide(values):
        parts = by_pattern(shared, values)
        pieces = [parts[i : i + 1] for i in range(5 * prims)]
        pieces += [jnp.zeros((1, rhs), jnp.float32)] * (wide_rows * chunks - 5 * prims)
        rows = [side(pieces[i * chunks : (i + 1) * chunks]) for i in range(wide_rows)]
        wide_all[me] = jnp.concatenate(rows, axis=0)
        send_all(wide_all, sems_of(ITERS - 1))

    def gather_wide():
        wait_others(wide_all, rest_recv.at[ITERS - 1])
        turned = [wide_all[:, i, :].T for i in range(wide_rows)]
        pieces = [
            turned[i // chunks][i % chunks * rhs : (i % chunks + 1) * rhs]
            for i in range(5 * prims)
        ]
        return total_of(side(pieces), hot[...])

    def mapped(total, maps, columns):
        high, low = split(total)
        both = dot(jnp.concatenate([high, low], axis=0), maps[0, :, :columns])
        return both[:rhs] + both[rhs:] + dot(high, maps[1, :, :columns])

    def correct(total, columns):
        return mapped(total, coarse, columns)

    def whole_inverse():
        each_wide(
            lambda other: pltpu.make_async_copy(
                inverse_all.at[other], inverse_all.at[other], inverse_recv.at[other]
            ).wait()
        )
        for w in range(wides):
            inverse_flat[w * owned : (w + 1) * owned, :] = inverse_all[w]

    def expand(values):
        return dot(chosen[...], jnp.concatenate(split3(values), axis=0))

    scaled = damping * weights

    def advanced(turn, base):
        change = scaled * side([face_out[turn, f] + face_in[turn, f] for f in faces])
        return change if base is None else base + change

    drain_faces(0)
    each_near(lambda f: basis_copy(f).wait_send())
    wait_faces(1)
    sol[...] = advanced(1, None)

    apply_schur(2, sol[...])
    wait_near(coarse_near, coarse_recv)
    effect = weights * side([coarse_out[f] + coarse_near[f] for f in faces])
    if small_mesh:
        high, low = split(effect)
        both = dot(jnp.concatenate([high, low], axis=0), neumann[...])
        for f, part in enumerate(cut(both[:order] + both[order:])):
            second_out[f] = part
        each_near(lambda f: second_copy(f).start())
        send_echo(effect)
        coarse[0], coarse[1] = split(side([spread_out[...], effect]))
    else:
        whole_inverse()
        both = side([spread_out[...], effect])
        coarse[0], coarse[1] = split(dot(inverse_flat[...], both, ((1,), (0,)), HIGHEST))
    fetch[5].wait()
    wanted = lax.broadcasted_iota(jnp.int32, (rhs, column.shape[1]), 0) == column[...]
    wanted = wanted.astype(jnp.float32).T.astype(jnp.bfloat16)
    chosen[...] = side([wanted, wanted, wanted])

    for iteration in range(1, ITERS):
        turn = 2 * iteration
        last = iteration == ITERS - 1
        if iteration > 1:
            apply_schur(turn, sol[...])
        if last and small_mesh:
            send_wide(side([face_out[turn, f] for f in faces]))
        deferred = small_mesh and iteration == 1
        if not deferred:
            solved = gather(iteration - 1)
            if small_mesh:
                echo = jnp.stack(split(gather_echo()))
                solved = mapped(solved - mapped(before, echo, order), inverse, order)
            before = solved
            change = correct(solved, 2 * inner)
            sol[...] += change[:, :inner]
        wait_faces(turn)
        residual = weighted(turn)
        if not deferred:
            residual = residual - change[:, inner:]
        apply_neumann(turn + 1, residual)
        if not (last and small_mesh):
            restrict(iteration, residual)
            send_all(rest_all.at[iteration], sems_of(iteration))
        drain_faces(turn - 1)
        drain_faces(turn)
        if last:
            each_near(lambda f: coarse_copy(f).wait_send())
            each_wide(lambda other: inverse_copy(other).wait_send())
            for i in range(ITERS - 1):
                wait_others(rest_all.at[i], rest_send.at[i])
            if small_mesh:
                each_near(lambda f: second_copy(f).wait_send())
                wait_others(echo_all, rest_send.at[ITERS])
                solved = mapped(gather_wide() - mapped(before, echo, order), inverse, order)
            else:
                solved = gather(iteration)
            change = correct(solved, inner)
            for f, part in enumerate(cut(expand(sol[...] + change))):
                out[f] = part
            wait_faces(turn + 1)
            for f, part in enumerate(cut(expand(advanced(turn + 1, None)))):
                out[f] = out[f] + part
        else:
            if small_mesh:
                wait_near(second_near, second_recv)
                later = scaled * side([second_out[f] + second_near[f] for f in faces])
                first[0], first[1] = split(spread_out[...] - later)
                whole_inverse()
                inverse = jnp.stack(split(inverse_flat[...]))
                solved = mapped(gather(0), inverse, order)
                before = solved
                sol[...] += mapped(solved, first, inner)
            wait_faces(turn + 1)
            sol[...] = advanced(turn + 1, sol[...])

    drain_faces(2 * ITERS - 1)
    if small_mesh:
        wait_others(wide_all, rest_send.at[ITERS - 1])
    else:
        wait_others(rest_all.at[ITERS - 1], rest_send.at[ITERS - 1])


def body(
    load_table, load_column, face_order, schur, neumann, coarse_basis, corner_map, coarse_inverse
):
    subs, wides = lax.axis_size("sub"), lax.axis_size("wide")
    devices = subs * wides
    patterns, width = load_table.shape[2], load_table.shape[4]
    rhs = load_column.shape[0]
    inner = schur.shape[2]
    prims = coarse_basis.shape[2]
    owned, order = coarse_inverse.shape
    assert schur.shape[0] == 1 and schur.shape[1] == 1
    f32, bf16 = jnp.float32, jnp.bfloat16
    group = min(devices, 32)
    dma = pltpu.SemaphoreType.DMA
    hbm = pl.BlockSpec(memory_space=pl.ANY)
    result = pl.pallas_call(
        functools.partial(kernel, (subs, wides)),
        out_shape=pltpu.VMEM((4, rhs, width), f32),
        in_specs=[hbm] * 8,
        out_specs=pl.BlockSpec(memory_space=pltpu.VMEM),
        scratch_shapes=[
            pltpu.SMEM((4,), face_order.dtype),
            pltpu.SMEM((prims,), corner_map.dtype),
            pltpu.VMEM((patterns * 4, width), load_table.dtype),
            pltpu.VMEM((prims * 4, width), coarse_basis.dtype),
            pltpu.VMEM((owned, order), f32),
            pltpu.VMEM((1, rhs), load_column.dtype),
            pltpu.VMEM((4, 4, width, width), schur.dtype),
            pltpu.VMEM((4, 4, width, width), neumann.dtype),
            pltpu.VMEM((inner, inner), schur.dtype),
            pltpu.VMEM((inner, inner), neumann.dtype),
            pltpu.VMEM((4, patterns, width), f32),
            pltpu.VMEM((patterns, 4 * width), f32),
            pltpu.VMEM((2 * ITERS, 4, patterns, width), f32),
            pltpu.VMEM((2 * ITERS, 4, patterns, width), f32),
            pltpu.VMEM((4, 2 * prims, width), f32),
            pltpu.VMEM((4, 2 * prims, width), f32),
            pltpu.VMEM((wides, owned, order), f32),
            pltpu.VMEM((order, order), f32),
            pltpu.VMEM((order, 4 * width), f32),
            pltpu.VMEM((5 * prims, 4 * width), f32),
            pltpu.VMEM((5 * group * prims, order if devices == group else LANES), bf16),
            pltpu.VMEM((rhs, 3 * patterns), bf16),
            pltpu.VMEM((2, order, 8 * width), bf16),
            pltpu.VMEM((4, order, width), f32),
            pltpu.VMEM((4, order, width), f32),
            pltpu.VMEM((2, order, 4 * width), bf16),
            pltpu.VMEM((4, order, width), f32),
            pltpu.VMEM((4, order, width), f32),
            pltpu.VMEM((ITERS, devices, 1, LANES), f32),
            pltpu.VMEM((group, -(-5 * prims * patterns // LANES), LANES), f32),
            pltpu.VMEM((group, prims // 2, LANES), f32),
            pltpu.SemaphoreType.REGULAR((3,)),
            dma((6,)),
            dma((2, 4)),
            dma((2 * ITERS, 4)),
            dma((2 * ITERS, 4)),
            dma((4,)),
            dma((4,)),
            dma((4,)),
            dma((4,)),
            dma((4,)),
            dma((4,)),
            dma((wides,)),
            dma((wides,)),
            dma((ITERS + 1,)),
            dma((ITERS + 1,)),
        ],
        compiler_params=pltpu.CompilerParams(
            collective_id=0, has_side_effects=True, vmem_limit_bytes=VMEM_LIMIT
        ),
        name="bddc",
    )(
        face_order.reshape(4),
        corner_map.reshape(prims),
        load_table.reshape(patterns * 4, width),
        coarse_basis.reshape(prims * 4, width),
        coarse_inverse,
        load_column.reshape(1, rhs),
        schur.reshape(4, width, inner),
        neumann.reshape(4, width, inner),
    )
    return result.reshape(1, 1, 4, rhs, width)


def solution(mesh):
    in_specs = (
        P("sub", "wide", None, None, None),
        P(),
        P("sub", "wide", None),
        P("sub", "wide", None, None),
        P("sub", "wide", None, None),
        P("sub", "wide", None, None, None),
        P("sub", "wide", None),
        P("wide", None),
    )
    out_specs = P("sub", "wide", None, None, None)
    return jax.shard_map(body, mesh=mesh, in_specs=in_specs, out_specs=out_specs, check_vma=False)
```

```python
import functools

import jax
import jax.numpy as jnp
from jax import lax
from jax.experimental import pallas as pl
from jax.experimental.pallas import tpu as pltpu
from jax.sharding import PartitionSpec as P

ITERS = 3
damping = 0.3
MESH = pl.DeviceIdType.MESH
HIGHEST = lax.Precision.HIGHEST
OPPOSITE = (1, 0, 3, 2)
LANES = 128
VMEM_LIMIT = 56 * 1024 * 1024


def split(value):
    high = value.astype(jnp.bfloat16)
    low = (value - high.astype(jnp.float32)).astype(jnp.bfloat16)
    return high, low


def split3(value):
    high, low = split(value)
    rest = value - high.astype(jnp.float32) - low.astype(jnp.float32)
    return high, low, rest.astype(jnp.bfloat16)


def dot(a, b, dims=((1,), (0,)), precision=None):
    return lax.dot_general(
        a, b, (dims, ((), ())), precision=precision, preferred_element_type=jnp.float32
    )


def kernel(
    sizes,
    face_order_hbm,
    corner_map_hbm,
    load_table_hbm,
    basis_hbm,
    inverse_hbm,
    column_hbm,
    schur_hbm,
    neumann_hbm,
    out,
    face_order,
    corner_map,
    load_table,
    basis_in,
    inverse_in,
    column,
    schur_in,
    neumann_in,
    schur,
    neumann,
    load,
    sol,
    face_out,
    face_in,
    basis_out,
    basis_near,
    inverse_all,
    inverse_flat,
    spread_out,
    gmat,
    hot,
    chosen,
    coarse,
    coarse_out,
    coarse_near,
    first,
    second_out,
    second_near,
    rest_all,
    wide_all,
    echo_all,
    far_sem,
    local_sem,
    block_sem,
    face_send,
    face_recv,
    basis_send,
    basis_recv,
    coarse_send,
    coarse_recv,
    second_send,
    second_recv,
    inverse_send,
    inverse_recv,
    rest_send,
    rest_recv,
):
    subs, wides = sizes
    devices = subs * wides
    rhs, width = load.shape[1], load.shape[2]
    inner = 4 * width
    prims = basis_out.shape[1] // 2
    order = inverse_flat.shape[0]
    owned = inverse_in.shape[0]
    group = min(devices, 32)
    marked = prims * rhs
    small_mesh = devices <= 32
    row = lax.axis_index("sub")
    col = lax.axis_index("wide")
    me = row * wides + col
    has = (row > 0, row < subs - 1, col > 0, col < wides - 1)
    near = ((row - 1, col), (row + 1, col), (row, col - 1), (row, col + 1))
    share = [jnp.where(flag, jnp.float32(0.5), jnp.float32(1.0)) for flag in has]
    faces = range(4)

    pairs = (
        (load_table_hbm, load_table),
        (basis_hbm, basis_in),
        (corner_map_hbm, corner_map),
        (face_order_hbm, face_order),
        (inverse_hbm, inverse_in),
        (column_hbm, column),
    )
    fetch = [
        pltpu.make_async_copy(source, target, local_sem.at[i])
        for i, (source, target) in enumerate(pairs)
    ]
    blocks = [
        [
            pltpu.make_async_copy(
                source.at[:, :, b * width : (b + 1) * width], target.at[b], sems.at[b]
            )
            for b in faces
        ]
        for source, target, sems in (
            (neumann_hbm, neumann_in, block_sem.at[0]),
            (schur_hbm, schur_in, block_sem.at[1]),
        )
    ]
    for copy in fetch[:3]:
        copy.start()

    def loop(first, last, action):
        if small_mesh:
            for step in range(first, last):
                action(step)
        else:

            def one(step, carry):
                action(step)
                return carry

            lax.fori_loop(first, last, one, 0)

    def each_wide(action):
        loop(1, wides, lambda step: action(lax.rem(col + step, wides)))

    def each_sub(action):
        loop(1, subs, lambda step: action(lax.rem(row + step, subs)))

    barrier = pltpu.get_barrier_semaphore()

    def signal(sem, where):
        pl.semaphore_signal(sem, inc=1, device_id=where, device_id_type=MESH)

    stepwise = subs <= 4 and wides <= 8
    near_by = [(-1, 0), (1, 0), (0, -1), (0, 1), (0, -3), (0, 3)]
    around = {(a + c, b + d) for a, b in near_by for c, d in near_by} | set(near_by)
    around = sorted(around - {(0, 0)})

    def present(steps):
        return [
            (
                jnp.logical_and(
                    jnp.logical_and(row + r >= 0, row + r < subs),
                    jnp.logical_and(col + c >= 0, col + c < wides),
                ),
                (row + r, col + c),
            )
            for r, c in steps
        ]

    known, known_twice = present(near_by), present(around)
    if stepwise:
        greeted = sum(flag.astype(jnp.int32) for flag, _ in known)
        greeted_twice = sum(flag.astype(jnp.int32) for flag, _ in known_twice)
    else:
        greeted = subs - 1 + wides - 1

    def greet(sem, those=known):
        for flag, where in those:

            @pl.when(flag)
            def _():
                signal(sem, where)

    if stepwise:
        greet(barrier)
    else:
        each_sub(lambda other: signal(barrier, (other, col)))
        each_wide(lambda other: signal(barrier, (row, other)))
    for copy in fetch[3:] + blocks[0] + blocks[1]:
        copy.start()

    def face_copy(turn, f):
        return pltpu.make_async_remote_copy(
            src_ref=face_out.at[turn, f],
            dst_ref=face_in.at[turn, OPPOSITE[f]],
            send_sem=face_send.at[turn, f],
            recv_sem=face_recv.at[turn, OPPOSITE[f]],
            device_id=near[f],
            device_id_type=MESH,
        )

    def to_near(source, target, send, recv, f):
        return pltpu.make_async_remote_copy(
            src_ref=source.at[f],
            dst_ref=target.at[OPPOSITE[f]],
            send_sem=send.at[f],
            recv_sem=recv.at[OPPOSITE[f]],
            device_id=near[f],
            device_id_type=MESH,
        )

    def basis_copy(f):
        return to_near(basis_out, basis_near, basis_send, basis_recv, f)

    def coarse_copy(f):
        return to_near(coarse_out, coarse_near, coarse_send, coarse_recv, f)

    def second_copy(f):
        return to_near(second_out, second_near, second_send, second_recv, f)

    def inverse_copy(other):
        return pltpu.make_async_remote_copy(
            src_ref=inverse_all.at[col],
            dst_ref=inverse_all.at[col],
            send_sem=inverse_send.at[other],
            recv_sem=inverse_recv.at[col],
            device_id=(row, other),
            device_id_type=MESH,
        )

    def spread_copy(blocks, sems, where):
        return pltpu.make_async_remote_copy(
            src_ref=blocks.at[me],
            dst_ref=blocks.at[me],
            send_sem=sems[0],
            recv_sem=sems[1],
            device_id=where,
            device_id_type=MESH,
        )

    def sems_of(i):
        return rest_send.at[i], rest_recv.at[i]

    def each_near(action):
        for f in faces:

            @pl.when(has[f])
            def _():
                action(f)

    def wait_near(target, recv):
        each_near(lambda f: pltpu.make_async_copy(target.at[f], target.at[f], recv.at[f]).wait())

    def wait_others(blocks, sem):
        others = blocks.at[pl.ds(0, devices - 1)]
        pltpu.make_async_copy(others, others, sem).wait()

    def send_faces(turn):
        each_near(lambda f: face_copy(turn, f).start())

    def wait_faces(turn):
        wait_near(face_in.at[turn], face_recv.at[turn])

    def drain_faces(turn):
        each_near(lambda f: face_copy(turn, f).wait_send())

    upper = row < (subs + 1) // 2
    half = subs // 2

    def send_all(blocks, sems):
        def rows(i):
            there = jnp.where(upper, subs - 1 - i, i)

            def columns(step):
                other = lax.rem(col + step, wides)

                def start():
                    spread_copy(blocks, sems, (there, other)).start()

                if isinstance(step, int) and (step > 0 or i < half):
                    start()
                else:
                    pl.when(jnp.logical_or(there != row, step != 0))(start)

            loop(0, wides, columns)

        loop(0, subs, rows)

    def side(values):
        return jnp.concatenate(values, axis=1)

    def cut(value):
        return [value[:, f * width : (f + 1) * width] for f in faces]

    def arranged(rows):
        target = 4 * lax.broadcasted_iota(jnp.int32, (rows, 4 * rows), 0)
        source = lax.broadcasted_iota(jnp.int32, (rows, 4 * rows), 1)
        picks = [(source == target + f).astype(jnp.float32) for f in faces]
        return jnp.concatenate(picks, axis=0).astype(jnp.bfloat16)

    table_picks = arranged(rhs)
    basis_picks = arranged(prims)
    weights = side([share[f] * jnp.ones((1, width), jnp.float32) for f in faces])

    fetch[0].wait()
    table = dot(table_picks, load_table[...])
    for f in faces:
        load[f] = table[f * rhs : (f + 1) * rhs]
        face_out[0, f] = table[f * rhs : (f + 1) * rhs]
    pl.semaphore_wait(barrier, greeted)
    send_faces(0)
    if stepwise:
        greet(far_sem.at[0])
    else:
        each_wide(lambda other: signal(far_sem.at[1], (row, other)))
    fetch[1].wait()
    fetch[2].wait()
    own = dot(basis_picks, basis_in[...])
    row_of = lax.broadcasted_iota(jnp.int32, (prims, width), 0)
    marks = jnp.zeros((prims, width), jnp.int32)
    for p in range(prims):
        marks = jnp.where(row_of == p, corner_map[p], marks)
    marks = marks.astype(jnp.float32)
    lane_of = lax.broadcasted_iota(jnp.int32, (1, LANES - marked), 1)
    mark_row = jnp.zeros((1, LANES - marked), jnp.int32)
    for p in range(prims):
        mark_row = jnp.where(lane_of == p, corner_map[p], mark_row)
    mark_row = mark_row.astype(jnp.float32)
    own_basis = side([own[f * prims : (f + 1) * prims] for f in faces]).astype(jnp.bfloat16)
    for f in faces:
        basis_out[f] = jnp.concatenate([own[f * prims : (f + 1) * prims], marks], axis=0)

    each_near(lambda f: basis_copy(f).start())

    for f in faces:

        @pl.when(jnp.logical_not(has[f]))
        def _():
            for turn in range(2 * ITERS):
                face_in[turn, f] = jnp.zeros((rhs, width), jnp.float32)
            basis_near[f] = jnp.zeros(basis_near.shape[1:], jnp.float32)
            coarse_near[f] = jnp.zeros(coarse_near.shape[1:], jnp.float32)
            second_near[f] = jnp.zeros(second_near.shape[1:], jnp.float32)

    fetch[3].wait()
    spot = []
    for f in faces:
        found = jnp.int32(0)
        for b in range(1, 4):
            found = jnp.where(face_order[b] == f, jnp.int32(b), found)
        spot.append(found)

    def by_face(source, target):
        for f in faces:
            for g in faces:
                target[f * width : (f + 1) * width, g * width : (g + 1) * width] = source[
                    spot[g], spot[f]
                ]

    for copy in blocks[0]:
        copy.wait()
    by_face(neumann_in, neumann)

    def weighted(turn):
        return side([share[f] * (face_out[turn, f] + face_in[turn, f]) for f in faces])

    def apply_neumann(turn, values):
        result = dot(values.astype(jnp.bfloat16), neumann[...])
        for f, part in enumerate(cut(result)):
            face_out[turn, f] = part
        send_faces(turn)

    def by_pattern(left, values):
        high, low = split(values)
        both = dot(left, jnp.concatenate([high, low], axis=0), ((1,), (1,)))
        return both[:, : values.shape[0]] + both[:, values.shape[0] :]

    def restrict(iteration, values):
        parts = by_pattern(own_basis, values)
        rest_all[iteration, me] = side([parts[p : p + 1] for p in range(prims)] + [mark_row])

    fetch[4].wait()
    inverse_all[col] = inverse_in[...]
    if stepwise:
        pl.semaphore_wait(far_sem.at[0], greeted)
        greet(far_sem.at[1], known_twice)
    wait_faces(0)
    residual = weighted(0)
    apply_neumann(1, residual)
    restrict(0, residual)
    if stepwise:
        pl.semaphore_wait(far_sem.at[1], greeted_twice)
        greet(far_sem.at[2], known_twice)

    wait_near(basis_near, basis_recv)
    gmat[...] = jnp.zeros(gmat.shape, jnp.float32)
    gmat[0:prims, :] = side([basis_out[f, :prims] for f in faces])
    for f in faces:
        gmat[(f + 1) * prims : (f + 2) * prims, f * width : (f + 1) * width] = basis_near[
            f, :prims
        ]
    shared = (gmat[...] * weights).astype(jnp.bfloat16)

    for copy in blocks[1]:
        copy.wait()
    by_face(schur_in, schur)
    lanes = lax.broadcasted_iota(jnp.int32, (prims, order), 1).astype(jnp.float32)
    picks = [marks[:, :1] == lanes]
    picks += [basis_near[f, prims:, :1] == lanes for f in faces]
    mine = jnp.concatenate([flag.astype(jnp.float32) for flag in picks], axis=0)
    dense = dot(mine.T.astype(jnp.bfloat16), gmat[...].astype(jnp.bfloat16))
    spread_out[...] = damping * weights * dense
    high, low = split(spread_out[...])
    both = dot(jnp.concatenate([high, low], axis=0), schur[...])
    effect = both[:order] + both[order:]
    for f, part in enumerate(cut(effect)):
        coarse_out[f] = part
    each_near(lambda f: coarse_copy(f).start())
    if stepwise:
        pl.semaphore_wait(far_sem.at[2], greeted_twice)
    else:
        pl.semaphore_wait(far_sem.at[1], wides - 1)
    send_all(rest_all.at[0], sems_of(0))
    each_wide(lambda other: inverse_copy(other).start())

    def apply_schur(turn, values, extra=None):
        high, low = split(values)
        halves = jnp.concatenate([high, low], axis=0)
        both = dot(halves, schur[...])
        for f, part in enumerate(cut(both[:rhs] + both[rhs:])):
            face_out[turn, f] = load[f] - part
        if extra is not None:
            both = dot(extra, halves, ((1,), (1,)))
            both = both[: 5 * prims] + both[5 * prims :]
            extra = both[:, :rhs] + both[:, rhs:]
        send_faces(turn)
        return extra

    def hot_of(part):
        numbers = rest_all[0, pl.ds(part * group, group), 0, :]
        lanes = lax.broadcasted_iota(jnp.int32, (group, order), 1).astype(jnp.float32)
        return numbers, [
            numbers[:, marked + p : marked + p + 1] == lanes for p in range(prims)
        ]

    def joined_hot(flags):
        return jnp.concatenate([flag.astype(jnp.float32) for flag in flags], axis=0).astype(
            jnp.bfloat16
        )

    def mark():
        numbers, flags = hot_of(0)
        for shift in (-wides, wides, -1, 1):
            cutoff = shift % devices
            moved = jnp.concatenate([numbers[cutoff:], numbers[:cutoff]], axis=0)
            lanes = lax.broadcasted_iota(jnp.int32, (group, order), 1).astype(jnp.float32)
            flags = flags + [
                moved[:, marked + p : marked + p + 1] == lanes for p in range(prims)
            ]
        hot[...] = joined_hot(flags)

    def total_of(rows, high_hot):
        high, low = split(rows)
        both = dot(jnp.concatenate([high, low], axis=0), high_hot)
        return both[: rows.shape[0]] + both[rows.shape[0] :]

    def gather(iteration):
        def one(part, own_hot):
            turned = rest_all[iteration, pl.ds(part * group, group), 0, :].T
            return total_of(side([turned[p * rhs : (p + 1) * rhs] for p in range(prims)]), own_hot)

        wait_others(rest_all.at[iteration], rest_recv.at[iteration])
        if small_mesh:
            if iteration == 0:
                mark()
            return one(0, hot[: prims * group])
        return lax.fori_loop(
            0,
            devices // group,
            lambda part, total: total + one(part, joined_hot(hot_of(part)[1])),
            jnp.zeros((rhs, order), jnp.float32),
        )

    def send_echo(values):
        parts = by_pattern(own_basis, values)
        blank = jnp.zeros((1, LANES - 2 * order), jnp.float32)
        rows = [side([parts[p : p + 1], parts[p + 1 : p + 2], blank]) for p in range(0, prims, 2)]
        echo_all[me] = jnp.concatenate(rows, axis=0)
        send_all(echo_all, sems_of(ITERS))

    def gather_echo():
        wait_others(echo_all, rest_recv.at[ITERS])
        turned = [echo_all[:, i, :].T for i in range(prims // 2)]
        pieces = [
            turned[p // 2][p % 2 * order : (p % 2 + 1) * order] for p in range(prims)
        ]
        return total_of(side(pieces), hot[: prims * group])

    chunks = LANES // rhs
    wide_rows = -(-5 * prims // chunks)

    def send_wide(parts):
        pieces = [parts[i : i + 1] for i in range(5 * prims)]
        pieces += [jnp.zeros((1, rhs), jnp.float32)] * (wide_rows * chunks - 5 * prims)
        rows = [side(pieces[i * chunks : (i + 1) * chunks]) for i in range(wide_rows)]
        wide_all[me] = jnp.concatenate(rows, axis=0)
        send_all(wide_all, sems_of(ITERS - 1))

    def gather_wide():
        wait_others(wide_all, rest_recv.at[ITERS - 1])
        turned = [wide_all[:, i, :].T for i in range(wide_rows)]
        pieces = [
            turned[i // chunks][i % chunks * rhs : (i % chunks + 1) * rhs]
            for i in range(5 * prims)
        ]
        return total_of(side(pieces), hot[...])

    def mapped(total, maps, columns):
        high, low = split(total)
        both = dot(jnp.concatenate([high, low], axis=0), maps[0, :, :columns])
        return both[:rhs] + both[rhs:] + dot(high, maps[1, :, :columns])

    def correct(total, columns):
        return mapped(total, coarse, columns)

    def whole_inverse():
        each_wide(
            lambda other: pltpu.make_async_copy(
                inverse_all.at[other], inverse_all.at[other], inverse_recv.at[other]
            ).wait()
        )
        for w in range(wides):
            inverse_flat[w * owned : (w + 1) * owned, :] = inverse_all[w]

    def expand(values):
        return dot(chosen[...], jnp.concatenate(split3(values), axis=0))

    scaled = damping * weights

    def advanced(turn, base):
        change = scaled * side([face_out[turn, f] + face_in[turn, f] for f in faces])
        return change if base is None else base + change

    drain_faces(0)
    each_near(lambda f: basis_copy(f).wait_send())
    wait_faces(1)
    sol[...] = advanced(1, None)

    apply_schur(2, sol[...])
    wait_near(coarse_near, coarse_recv)
    effect = weights * side([coarse_out[f] + coarse_near[f] for f in faces])
    if small_mesh:
        high, low = split(effect)
        both = dot(jnp.concatenate([high, low], axis=0), neumann[...])
        for f, part in enumerate(cut(both[:order] + both[order:])):
            second_out[f] = part
        each_near(lambda f: second_copy(f).start())
        send_echo(effect)
        coarse[0], coarse[1] = split(side([spread_out[...], effect]))
    else:
        whole_inverse()
        both = side([spread_out[...], effect])
        coarse[0], coarse[1] = split(dot(inverse_flat[...], both, ((1,), (0,)), HIGHEST))
    fetch[5].wait()
    wanted = lax.broadcasted_iota(jnp.int32, (rhs, column.shape[1]), 0) == column[...]
    wanted = wanted.astype(jnp.float32).T.astype(jnp.bfloat16)
    chosen[...] = side([wanted, wanted, wanted])

    for iteration in range(1, ITERS):
        turn = 2 * iteration
        last = iteration == ITERS - 1
        if last and small_mesh:
            send_wide(load_parts - apply_schur(turn, sol[...], schur_parts))
        elif iteration > 1:
            apply_schur(turn, sol[...])
        deferred = small_mesh and iteration == 1
        if not deferred:
            if small_mesh:
                echo = jnp.stack(split(gather_echo()))
                taken = mapped(before, echo, order)
                ends = jnp.concatenate([inverse[0], inverse[1]], axis=0)
                both = dot(ends, side([coarse[0], coarse[1]]))
                both = both[:order] + both[order:]
                coarse[0], coarse[1] = split(both[:, : 2 * inner] + both[:, 2 * inner :])
                solved = gather(iteration - 1) - taken
            else:
                solved = gather(iteration - 1)
            change = correct(solved, 2 * inner)
            sol[...] += change[:, :inner]
        wait_faces(turn)
        residual = weighted(turn)
        if not deferred:
            residual = residual - change[:, inner:]
        apply_neumann(turn + 1, residual)
        if not (last and small_mesh):
            restrict(iteration, residual)
            send_all(rest_all.at[iteration], sems_of(iteration))
        drain_faces(turn - 1)
        drain_faces(turn)
        if last:
            each_near(lambda f: coarse_copy(f).wait_send())
            each_wide(lambda other: inverse_copy(other).wait_send())
            for i in range(ITERS - 1):
                wait_others(rest_all.at[i], rest_send.at[i])
            if small_mesh:
                each_near(lambda f: second_copy(f).wait_send())
                wait_others(echo_all, rest_send.at[ITERS])
                before = mapped(solved, inverse, order)
                taken = mapped(before, echo, order)
            for f, part in enumerate(cut(expand(sol[...]))):
                out[f] = part
            if small_mesh:
                change = correct(gather_wide() - taken, inner)
            else:
                change = correct(gather(iteration), inner)
            wait_faces(turn + 1)
            for f, part in enumerate(cut(expand(advanced(turn + 1, change)))):
                out[f] = out[f] + part
        else:
            if small_mesh:
                schur_parts = jnp.concatenate(split(dot(shared, schur[...])), axis=0)
                load_parts = by_pattern(shared, side([load[f] for f in faces]))
                wait_near(second_near, second_recv)
                later = scaled * side([second_out[f] + second_near[f] for f in faces])
                first[0], first[1] = split(spread_out[...] - later)
                whole_inverse()
                inverse = jnp.stack(split(inverse_flat[...]))
                solved = mapped(gather(0), inverse, order)
                before = solved
                sol[...] += mapped(solved, first, inner)
            wait_faces(turn + 1)
            sol[...] = advanced(turn + 1, sol[...])

    drain_faces(2 * ITERS - 1)
    if small_mesh:
        wait_others(wide_all, rest_send.at[ITERS - 1])
    else:
        wait_others(rest_all.at[ITERS - 1], rest_send.at[ITERS - 1])


def body(
    load_table, load_column, face_order, schur, neumann, coarse_basis, corner_map, coarse_inverse
):
    subs, wides = lax.axis_size("sub"), lax.axis_size("wide")
    devices = subs * wides
    patterns, width = load_table.shape[2], load_table.shape[4]
    rhs = load_column.shape[0]
    inner = schur.shape[2]
    prims = coarse_basis.shape[2]
    owned, order = coarse_inverse.shape
    assert schur.shape[0] == 1 and schur.shape[1] == 1
    f32, bf16 = jnp.float32, jnp.bfloat16
    group = min(devices, 32)
    dma = pltpu.SemaphoreType.DMA
    hbm = pl.BlockSpec(memory_space=pl.ANY)
    result = pl.pallas_call(
        functools.partial(kernel, (subs, wides)),
        out_shape=pltpu.VMEM((4, rhs, width), f32),
        in_specs=[hbm] * 8,
        out_specs=pl.BlockSpec(memory_space=pltpu.VMEM),
        scratch_shapes=[
            pltpu.SMEM((4,), face_order.dtype),
            pltpu.SMEM((prims,), corner_map.dtype),
            pltpu.VMEM((patterns * 4, width), load_table.dtype),
            pltpu.VMEM((prims * 4, width), coarse_basis.dtype),
            pltpu.VMEM((owned, order), f32),
            pltpu.VMEM((1, rhs), load_column.dtype),
            pltpu.VMEM((4, 4, width, width), schur.dtype),
            pltpu.VMEM((4, 4, width, width), neumann.dtype),
            pltpu.VMEM((inner, inner), schur.dtype),
            pltpu.VMEM((inner, inner), neumann.dtype),
            pltpu.VMEM((4, patterns, width), f32),
            pltpu.VMEM((patterns, 4 * width), f32),
            pltpu.VMEM((2 * ITERS, 4, patterns, width), f32),
            pltpu.VMEM((2 * ITERS, 4, patterns, width), f32),
            pltpu.VMEM((4, 2 * prims, width), f32),
            pltpu.VMEM((4, 2 * prims, width), f32),
            pltpu.VMEM((wides, owned, order), f32),
            pltpu.VMEM((order, order), f32),
            pltpu.VMEM((order, 4 * width), f32),
            pltpu.VMEM((5 * prims, 4 * width), f32),
            pltpu.VMEM((5 * group * prims, order if devices == group else LANES), bf16),
            pltpu.VMEM((rhs, 3 * patterns), bf16),
            pltpu.VMEM((2, order, 8 * width), bf16),
            pltpu.VMEM((4, order, width), f32),
            pltpu.VMEM((4, order, width), f32),
            pltpu.VMEM((2, order, 4 * width), bf16),
            pltpu.VMEM((4, order, width), f32),
            pltpu.VMEM((4, order, width), f32),
            pltpu.VMEM((ITERS, devices, 1, LANES), f32),
            pltpu.VMEM((group, -(-5 * prims * patterns // LANES), LANES), f32),
            pltpu.VMEM((group, prims // 2, LANES), f32),
            pltpu.SemaphoreType.REGULAR((3,)),
            dma((6,)),
            dma((2, 4)),
            dma((2 * ITERS, 4)),
            dma((2 * ITERS, 4)),
            dma((4,)),
            dma((4,)),
            dma((4,)),
            dma((4,)),
            dma((4,)),
            dma((4,)),
            dma((wides,)),
            dma((wides,)),
            dma((ITERS + 1,)),
            dma((ITERS + 1,)),
        ],
        compiler_params=pltpu.CompilerParams(
            collective_id=0, has_side_effects=True, vmem_limit_bytes=VMEM_LIMIT
        ),
        name="bddc",
    )(
        face_order.reshape(4),
        corner_map.reshape(prims),
        load_table.reshape(patterns * 4, width),
        coarse_basis.reshape(prims * 4, width),
        coarse_inverse,
        load_column.reshape(1, rhs),
        schur.reshape(4, width, inner),
        neumann.reshape(4, width, inner),
    )
    return result.reshape(1, 1, 4, rhs, width)


def solution(mesh):
    in_specs = (
        P("sub", "wide", None, None, None),
        P(),
        P("sub", "wide", None),
        P("sub", "wide", None, None),
        P("sub", "wide", None, None),
        P("sub", "wide", None, None, None),
        P("sub", "wide", None),
        P("wide", None),
    )
    out_specs = P("sub", "wide", None, None, None)
    return jax.shard_map(body, mesh=mesh, in_specs=in_specs, out_specs=out_specs, check_vma=False)
```

```python
import functools

import jax
import jax.numpy as jnp
from jax import lax
from jax.experimental import pallas as pl
from jax.experimental.pallas import tpu as pltpu
from jax.sharding import PartitionSpec as P

ITERS = 3
damping = 0.3
MESH = pl.DeviceIdType.MESH
HIGHEST = lax.Precision.HIGHEST
OPPOSITE = (1, 0, 3, 2)
LANES = 128
VMEM_LIMIT = 56 * 1024 * 1024


def split(value):
    high = value.astype(jnp.bfloat16)
    low = (value - high.astype(jnp.float32)).astype(jnp.bfloat16)
    return high, low


def split3(value):
    high, low = split(value)
    rest = value - high.astype(jnp.float32) - low.astype(jnp.float32)
    return high, low, rest.astype(jnp.bfloat16)


def dot(a, b, dims=((1,), (0,)), precision=None):
    return lax.dot_general(
        a, b, (dims, ((), ())), precision=precision, preferred_element_type=jnp.float32
    )


def kernel(
    sizes,
    face_order_hbm,
    corner_map_hbm,
    load_table_hbm,
    basis_hbm,
    inverse_hbm,
    column_hbm,
    schur_hbm,
    neumann_hbm,
    out,
    face_order,
    corner_map,
    load_table,
    basis_in,
    inverse_in,
    column,
    schur_in,
    neumann_in,
    schur,
    neumann,
    load,
    sol,
    face_out,
    face_in,
    basis_out,
    basis_near,
    inverse_all,
    inverse_flat,
    spread_out,
    gmat,
    hot,
    chosen,
    coarse,
    coarse_out,
    coarse_near,
    first,
    second_out,
    second_near,
    rest_all,
    wide_all,
    echo_all,
    far_sem,
    local_sem,
    block_sem,
    face_send,
    face_recv,
    basis_send,
    basis_recv,
    coarse_send,
    coarse_recv,
    second_send,
    second_recv,
    inverse_send,
    inverse_recv,
    rest_send,
    rest_recv,
):
    subs, wides = sizes
    devices = subs * wides
    rhs, width = load.shape[1], load.shape[2]
    inner = 4 * width
    prims = basis_out.shape[1] // 2
    order = inverse_flat.shape[0]
    owned = inverse_in.shape[0]
    group = min(devices, 32)
    marked = prims * rhs
    small_mesh = devices <= 32
    row = lax.axis_index("sub")
    col = lax.axis_index("wide")
    me = row * wides + col
    has = (row > 0, row < subs - 1, col > 0, col < wides - 1)
    near = ((row - 1, col), (row + 1, col), (row, col - 1), (row, col + 1))
    share = [jnp.where(flag, jnp.float32(0.5), jnp.float32(1.0)) for flag in has]
    faces = range(4)

    pairs = (
        (load_table_hbm, load_table),
        (basis_hbm, basis_in),
        (corner_map_hbm, corner_map),
        (face_order_hbm, face_order),
        (inverse_hbm, inverse_in),
        (column_hbm, column),
    )
    fetch = [
        pltpu.make_async_copy(source, target, local_sem.at[i])
        for i, (source, target) in enumerate(pairs)
    ]
    blocks = [
        [
            pltpu.make_async_copy(
                source.at[:, :, b * width : (b + 1) * width], target.at[b], sems.at[b]
            )
            for b in faces
        ]
        for source, target, sems in (
            (neumann_hbm, neumann_in, block_sem.at[0]),
            (schur_hbm, schur_in, block_sem.at[1]),
        )
    ]
    for copy in fetch[:3]:
        copy.start()

    def loop(first, last, action):
        if small_mesh:
            for step in range(first, last):
                action(step)
        else:

            def one(step, carry):
                action(step)
                return carry

            lax.fori_loop(first, last, one, 0)

    def each_wide(action):
        loop(1, wides, lambda step: action(lax.rem(col + step, wides)))

    def each_sub(action):
        loop(1, subs, lambda step: action(lax.rem(row + step, subs)))

    barrier = pltpu.get_barrier_semaphore()

    def signal(sem, where):
        pl.semaphore_signal(sem, inc=1, device_id=where, device_id_type=MESH)

    stepwise = subs <= 4 and wides <= 8
    near_by = [(-1, 0), (1, 0), (0, -1), (0, 1), (0, -3), (0, 3)]
    around = {(a + c, b + d) for a, b in near_by for c, d in near_by} | set(near_by)
    around = sorted(around - {(0, 0)})

    def present(steps):
        return [
            (
                jnp.logical_and(
                    jnp.logical_and(row + r >= 0, row + r < subs),
                    jnp.logical_and(col + c >= 0, col + c < wides),
                ),
                (row + r, col + c),
            )
            for r, c in steps
        ]

    known, known_twice = present(near_by), present(around)
    if stepwise:
        greeted = sum(flag.astype(jnp.int32) for flag, _ in known)
        greeted_twice = sum(flag.astype(jnp.int32) for flag, _ in known_twice)
    else:
        greeted = subs - 1 + wides - 1

    def greet(sem, those=known):
        for flag, where in those:

            @pl.when(flag)
            def _():
                signal(sem, where)

    if stepwise:
        greet(barrier)
    else:
        each_sub(lambda other: signal(barrier, (other, col)))
        each_wide(lambda other: signal(barrier, (row, other)))
    for copy in fetch[3:] + blocks[0] + blocks[1]:
        copy.start()

    def face_copy(turn, f):
        return pltpu.make_async_remote_copy(
            src_ref=face_out.at[turn, f],
            dst_ref=face_in.at[turn, OPPOSITE[f]],
            send_sem=face_send.at[turn, f],
            recv_sem=face_recv.at[turn, OPPOSITE[f]],
            device_id=near[f],
            device_id_type=MESH,
        )

    def to_near(source, target, send, recv, f):
        return pltpu.make_async_remote_copy(
            src_ref=source.at[f],
            dst_ref=target.at[OPPOSITE[f]],
            send_sem=send.at[f],
            recv_sem=recv.at[OPPOSITE[f]],
            device_id=near[f],
            device_id_type=MESH,
        )

    def basis_copy(f):
        return to_near(basis_out, basis_near, basis_send, basis_recv, f)

    def coarse_copy(f):
        return to_near(coarse_out, coarse_near, coarse_send, coarse_recv, f)

    def second_copy(f):
        return to_near(second_out, second_near, second_send, second_recv, f)

    def inverse_copy(other):
        return pltpu.make_async_remote_copy(
            src_ref=inverse_all.at[col],
            dst_ref=inverse_all.at[col],
            send_sem=inverse_send.at[other],
            recv_sem=inverse_recv.at[col],
            device_id=(row, other),
            device_id_type=MESH,
        )

    def spread_copy(blocks, sems, where):
        return pltpu.make_async_remote_copy(
            src_ref=blocks.at[me],
            dst_ref=blocks.at[me],
            send_sem=sems[0],
            recv_sem=sems[1],
            device_id=where,
            device_id_type=MESH,
        )

    def sems_of(i):
        return rest_send.at[i], rest_recv.at[i]

    def each_near(action):
        for f in faces:

            @pl.when(has[f])
            def _():
                action(f)

    def wait_near(target, recv):
        each_near(lambda f: pltpu.make_async_copy(target.at[f], target.at[f], recv.at[f]).wait())

    def wait_others(blocks, sem):
        others = blocks.at[pl.ds(0, devices - 1)]
        pltpu.make_async_copy(others, others, sem).wait()

    def send_faces(turn):
        each_near(lambda f: face_copy(turn, f).start())

    def wait_faces(turn):
        wait_near(face_in.at[turn], face_recv.at[turn])

    def drain_faces(turn):
        each_near(lambda f: face_copy(turn, f).wait_send())

    upper = row < (subs + 1) // 2
    half = subs // 2

    def send_all(blocks, sems):
        def rows(i):
            there = jnp.where(upper, subs - 1 - i, i)

            def columns(step):
                other = lax.rem(col + step, wides)

                def start():
                    spread_copy(blocks, sems, (there, other)).start()

                if isinstance(step, int) and (step > 0 or i < half):
                    start()
                else:
                    pl.when(jnp.logical_or(there != row, step != 0))(start)

            loop(0, wides, columns)

        loop(0, subs, rows)

    def side(values):
        return jnp.concatenate(values, axis=1)

    def cut(value):
        return [value[:, f * width : (f + 1) * width] for f in faces]

    def arranged(rows):
        target = 4 * lax.broadcasted_iota(jnp.int32, (rows, 4 * rows), 0)
        source = lax.broadcasted_iota(jnp.int32, (rows, 4 * rows), 1)
        picks = [(source == target + f).astype(jnp.float32) for f in faces]
        return jnp.concatenate(picks, axis=0).astype(jnp.bfloat16)

    table_picks = arranged(rhs)
    basis_picks = arranged(prims)
    weights = side([share[f] * jnp.ones((1, width), jnp.float32) for f in faces])

    fetch[0].wait()
    table = dot(table_picks, load_table[...])
    for f in faces:
        load[f] = table[f * rhs : (f + 1) * rhs]
        face_out[0, f] = table[f * rhs : (f + 1) * rhs]
    pl.semaphore_wait(barrier, greeted)
    send_faces(0)
    if stepwise:
        greet(far_sem.at[0])
    else:
        each_wide(lambda other: signal(far_sem.at[1], (row, other)))
    fetch[1].wait()
    fetch[2].wait()
    own = dot(basis_picks, basis_in[...])
    row_of = lax.broadcasted_iota(jnp.int32, (prims, width), 0)
    marks = jnp.zeros((prims, width), jnp.int32)
    for p in range(prims):
        marks = jnp.where(row_of == p, corner_map[p], marks)
    marks = marks.astype(jnp.float32)
    lane_of = lax.broadcasted_iota(jnp.int32, (1, LANES - marked), 1)
    mark_row = jnp.zeros((1, LANES - marked), jnp.int32)
    for p in range(prims):
        mark_row = jnp.where(lane_of == p, corner_map[p], mark_row)
    mark_row = mark_row.astype(jnp.float32)
    own_basis = side([own[f * prims : (f + 1) * prims] for f in faces]).astype(jnp.bfloat16)
    for f in faces:
        basis_out[f] = jnp.concatenate([own[f * prims : (f + 1) * prims], marks], axis=0)

    each_near(lambda f: basis_copy(f).start())

    for f in faces:

        @pl.when(jnp.logical_not(has[f]))
        def _():
            for turn in range(2 * ITERS):
                face_in[turn, f] = jnp.zeros((rhs, width), jnp.float32)
            basis_near[f] = jnp.zeros(basis_near.shape[1:], jnp.float32)
            coarse_near[f] = jnp.zeros(coarse_near.shape[1:], jnp.float32)
            second_near[f] = jnp.zeros(second_near.shape[1:], jnp.float32)

    fetch[3].wait()
    spot = []
    for f in faces:
        found = jnp.int32(0)
        for b in range(1, 4):
            found = jnp.where(face_order[b] == f, jnp.int32(b), found)
        spot.append(found)

    def by_face(source, target):
        for f in faces:
            for g in faces:
                target[f * width : (f + 1) * width, g * width : (g + 1) * width] = source[
                    spot[g], spot[f]
                ]

    for copy in blocks[0]:
        copy.wait()
    by_face(neumann_in, neumann)

    def weighted(turn):
        return side([share[f] * (face_out[turn, f] + face_in[turn, f]) for f in faces])

    def apply_neumann(turn, values):
        result = dot(values.astype(jnp.bfloat16), neumann[...])
        for f, part in enumerate(cut(result)):
            face_out[turn, f] = part
        send_faces(turn)

    def by_pattern(left, values):
        high, low = split(values)
        both = dot(left, jnp.concatenate([high, low], axis=0), ((1,), (1,)))
        return both[:, : values.shape[0]] + both[:, values.shape[0] :]

    def restrict(iteration, values):
        parts = by_pattern(own_basis, values)
        rest_all[iteration, me] = side([parts[p : p + 1] for p in range(prims)] + [mark_row])

    fetch[4].wait()
    inverse_all[col] = inverse_in[...]
    if stepwise:
        pl.semaphore_wait(far_sem.at[0], greeted)
        greet(far_sem.at[1], known_twice)
    wait_faces(0)
    residual = weighted(0)
    apply_neumann(1, residual)
    restrict(0, residual)
    if stepwise:
        pl.semaphore_wait(far_sem.at[1], greeted_twice)
        greet(far_sem.at[2], known_twice)

    wait_near(basis_near, basis_recv)
    gmat[...] = jnp.zeros(gmat.shape, jnp.float32)
    gmat[0:prims, :] = side([basis_out[f, :prims] for f in faces])
    for f in faces:
        gmat[(f + 1) * prims : (f + 2) * prims, f * width : (f + 1) * width] = basis_near[
            f, :prims
        ]
    shared = (gmat[...] * weights).astype(jnp.bfloat16)

    for copy in blocks[1]:
        copy.wait()
    by_face(schur_in, schur)
    lanes = lax.broadcasted_iota(jnp.int32, (prims, order), 1).astype(jnp.float32)
    picks = [marks[:, :1] == lanes]
    picks += [basis_near[f, prims:, :1] == lanes for f in faces]
    mine = jnp.concatenate([flag.astype(jnp.float32) for flag in picks], axis=0)
    dense = dot(mine.T.astype(jnp.bfloat16), gmat[...].astype(jnp.bfloat16))
    spread_out[...] = damping * weights * dense
    high, low = split(spread_out[...])
    both = dot(jnp.concatenate([high, low], axis=0), schur[...])
    effect = both[:order] + both[order:]
    for f, part in enumerate(cut(effect)):
        coarse_out[f] = part
    each_near(lambda f: coarse_copy(f).start())
    if stepwise:
        pl.semaphore_wait(far_sem.at[2], greeted_twice)
    else:
        pl.semaphore_wait(far_sem.at[1], wides - 1)
    send_all(rest_all.at[0], sems_of(0))
    each_wide(lambda other: inverse_copy(other).start())

    def apply_schur(turn, values, extra=None):
        high, low = split(values)
        halves = jnp.concatenate([high, low], axis=0)
        both = dot(halves, schur[...])
        for f, part in enumerate(cut(both[:rhs] + both[rhs:])):
            face_out[turn, f] = load[f] - part
        if extra is not None:
            both = dot(extra, halves, ((1,), (1,)))
            both = both[: 5 * prims] + both[5 * prims :]
            extra = both[:, :rhs] + both[:, rhs:]
        send_faces(turn)
        return extra

    def hot_of(part):
        numbers = rest_all[0, pl.ds(part * group, group), 0, :]
        lanes = lax.broadcasted_iota(jnp.int32, (group, order), 1).astype(jnp.float32)
        return numbers, [
            numbers[:, marked + p : marked + p + 1] == lanes for p in range(prims)
        ]

    def joined_hot(flags):
        return jnp.concatenate([flag.astype(jnp.float32) for flag in flags], axis=0).astype(
            jnp.bfloat16
        )

    def mark():
        numbers, flags = hot_of(0)
        for shift in (-wides, wides, -1, 1):
            cutoff = shift % devices
            moved = jnp.concatenate([numbers[cutoff:], numbers[:cutoff]], axis=0)
            lanes = lax.broadcasted_iota(jnp.int32, (group, order), 1).astype(jnp.float32)
            flags = flags + [
                moved[:, marked + p : marked + p + 1] == lanes for p in range(prims)
            ]
        hot[...] = joined_hot(flags)

    def total_of(rows, high_hot):
        high, low = split(rows)
        both = dot(jnp.concatenate([high, low], axis=0), high_hot)
        return both[: rows.shape[0]] + both[rows.shape[0] :]

    def gather(iteration):
        def one(part, own_hot):
            turned = rest_all[iteration, pl.ds(part * group, group), 0, :].T
            return total_of(side([turned[p * rhs : (p + 1) * rhs] for p in range(prims)]), own_hot)

        wait_others(rest_all.at[iteration], rest_recv.at[iteration])
        if small_mesh:
            if iteration == 0:
                mark()
            return one(0, hot[: prims * group])
        return lax.fori_loop(
            0,
            devices // group,
            lambda part, total: total + one(part, joined_hot(hot_of(part)[1])),
            jnp.zeros((rhs, order), jnp.float32),
        )

    def send_echo(values):
        parts = by_pattern(own_basis, values)
        blank = jnp.zeros((1, LANES - 2 * order), jnp.float32)
        rows = [side([parts[p : p + 1], parts[p + 1 : p + 2], blank]) for p in range(0, prims, 2)]
        echo_all[me] = jnp.concatenate(rows, axis=0)
        send_all(echo_all, sems_of(ITERS))

    def gather_echo():
        wait_others(echo_all, rest_recv.at[ITERS])
        turned = [echo_all[:, i, :].T for i in range(prims // 2)]
        pieces = [
            turned[p // 2][p % 2 * order : (p % 2 + 1) * order] for p in range(prims)
        ]
        return total_of(side(pieces), hot[: prims * group])

    chunks = LANES // rhs
    wide_rows = -(-5 * prims // chunks)

    def send_wide(parts):
        pieces = [parts[i : i + 1] for i in range(5 * prims)]
        pieces += [jnp.zeros((1, rhs), jnp.float32)] * (wide_rows * chunks - 5 * prims)
        rows = [side(pieces[i * chunks : (i + 1) * chunks]) for i in range(wide_rows)]
        wide_all[me] = jnp.concatenate(rows, axis=0)
        send_all(wide_all, sems_of(ITERS - 1))

    def gather_wide():
        wait_others(wide_all, rest_recv.at[ITERS - 1])
        turned = [wide_all[:, i, :].T for i in range(wide_rows)]
        pieces = [
            turned[i // chunks][i % chunks * rhs : (i % chunks + 1) * rhs]
            for i in range(5 * prims)
        ]
        return total_of(side(pieces), hot[...])

    def mapped(total, maps, columns):
        high, low = split(total)
        both = dot(jnp.concatenate([high, low], axis=0), maps[0, :, :columns])
        return both[:rhs] + both[rhs:] + dot(high, maps[1, :, :columns])

    def correct(total, columns):
        return mapped(total, coarse, columns)

    def whole_inverse():
        each_wide(
            lambda other: pltpu.make_async_copy(
                inverse_all.at[other], inverse_all.at[other], inverse_recv.at[other]
            ).wait()
        )
        for w in range(wides):
            inverse_flat[w * owned : (w + 1) * owned, :] = inverse_all[w]

    def expand(values, pieces=split3):
        values = jnp.concatenate(pieces(values), axis=0)
        return dot(chosen[:, : values.shape[0]], values)

    scaled = damping * weights

    def advanced(turn, base):
        change = scaled * side([face_out[turn, f] + face_in[turn, f] for f in faces])
        return change if base is None else base + change

    drain_faces(0)
    each_near(lambda f: basis_copy(f).wait_send())
    wait_faces(1)
    sol[...] = advanced(1, None)

    apply_schur(2, sol[...])
    wait_near(coarse_near, coarse_recv)
    effect = weights * side([coarse_out[f] + coarse_near[f] for f in faces])
    if small_mesh:
        high, low = split(effect)
        both = dot(jnp.concatenate([high, low], axis=0), neumann[...])
        for f, part in enumerate(cut(both[:order] + both[order:])):
            second_out[f] = part
        each_near(lambda f: second_copy(f).start())
        send_echo(effect)
        coarse[0], coarse[1] = split(side([spread_out[...], effect]))
    else:
        whole_inverse()
        both = side([spread_out[...], effect])
        coarse[0], coarse[1] = split(dot(inverse_flat[...], both, ((1,), (0,)), HIGHEST))
    fetch[5].wait()
    wanted = lax.broadcasted_iota(jnp.int32, (rhs, column.shape[1]), 0) == column[...]
    wanted = wanted.astype(jnp.float32).T.astype(jnp.bfloat16)
    chosen[...] = side([wanted, wanted, wanted])

    for iteration in range(1, ITERS):
        turn = 2 * iteration
        last = iteration == ITERS - 1
        if last and small_mesh:
            send_wide(load_parts - apply_schur(turn, sol[...], schur_parts))
        elif iteration > 1:
            apply_schur(turn, sol[...])
        deferred = small_mesh and iteration == 1
        if not deferred:
            if small_mesh:
                echo = jnp.stack(split(gather_echo()))
                taken = mapped(before, echo, order)
                ends = jnp.concatenate([inverse[0], inverse[1]], axis=0)
                both = dot(ends, side([coarse[0], coarse[1]]))
                both = both[:order] + both[order:]
                coarse[0], coarse[1] = split(both[:, : 2 * inner] + both[:, 2 * inner :])
                solved = gather(iteration - 1) - taken
            else:
                solved = gather(iteration - 1)
            change = correct(solved, 2 * inner)
            sol[...] += change[:, :inner]
        wait_faces(turn)
        residual = weighted(turn)
        if not deferred:
            residual = residual - change[:, inner:]
        apply_neumann(turn + 1, residual)
        if not (last and small_mesh):
            restrict(iteration, residual)
            send_all(rest_all.at[iteration], sems_of(iteration))
        drain_faces(turn - 1)
        drain_faces(turn)
        if last:
            each_near(lambda f: coarse_copy(f).wait_send())
            each_wide(lambda other: inverse_copy(other).wait_send())
            for i in range(ITERS - 1):
                wait_others(rest_all.at[i], rest_send.at[i])
            if small_mesh:
                each_near(lambda f: second_copy(f).wait_send())
                wait_others(echo_all, rest_send.at[ITERS])
                before = mapped(solved, inverse, order)
                taken = mapped(before, echo, order)
            for f, part in enumerate(cut(expand(sol[...]))):
                out[f] = part
            if small_mesh:
                change = correct(gather_wide() - taken, inner)
            else:
                change = correct(gather(iteration), inner)
            wait_faces(turn + 1)
            for f, part in enumerate(cut(expand(advanced(turn + 1, None) + change, split))):
                out[f] = out[f] + part
        else:
            if small_mesh:
                schur_parts = jnp.concatenate(split(dot(shared, schur[...])), axis=0)
                load_parts = by_pattern(shared, side([load[f] for f in faces]))
                wait_near(second_near, second_recv)
                later = scaled * side([second_out[f] + second_near[f] for f in faces])
                first[0], first[1] = split(spread_out[...] - later)
                whole_inverse()
                inverse = jnp.stack(split(inverse_flat[...]))
                solved = mapped(gather(0), inverse, order)
                before = solved
                sol[...] += mapped(solved, first, inner)
            wait_faces(turn + 1)
            sol[...] = advanced(turn + 1, sol[...])

    drain_faces(2 * ITERS - 1)
    if small_mesh:
        wait_others(wide_all, rest_send.at[ITERS - 1])
    else:
        wait_others(rest_all.at[ITERS - 1], rest_send.at[ITERS - 1])


def body(
    load_table, load_column, face_order, schur, neumann, coarse_basis, corner_map, coarse_inverse
):
    subs, wides = lax.axis_size("sub"), lax.axis_size("wide")
    devices = subs * wides
    patterns, width = load_table.shape[2], load_table.shape[4]
    rhs = load_column.shape[0]
    inner = schur.shape[2]
    prims = coarse_basis.shape[2]
    owned, order = coarse_inverse.shape
    assert schur.shape[0] == 1 and schur.shape[1] == 1
    f32, bf16 = jnp.float32, jnp.bfloat16
    group = min(devices, 32)
    dma = pltpu.SemaphoreType.DMA
    hbm = pl.BlockSpec(memory_space=pl.ANY)
    result = pl.pallas_call(
        functools.partial(kernel, (subs, wides)),
        out_shape=pltpu.VMEM((4, rhs, width), f32),
        in_specs=[hbm] * 8,
        out_specs=pl.BlockSpec(memory_space=pltpu.VMEM),
        scratch_shapes=[
            pltpu.SMEM((4,), face_order.dtype),
            pltpu.SMEM((prims,), corner_map.dtype),
            pltpu.VMEM((patterns * 4, width), load_table.dtype),
            pltpu.VMEM((prims * 4, width), coarse_basis.dtype),
            pltpu.VMEM((owned, order), f32),
            pltpu.VMEM((1, rhs), load_column.dtype),
            pltpu.VMEM((4, 4, width, width), schur.dtype),
            pltpu.VMEM((4, 4, width, width), neumann.dtype),
            pltpu.VMEM((inner, inner), schur.dtype),
            pltpu.VMEM((inner, inner), neumann.dtype),
            pltpu.VMEM((4, patterns, width), f32),
            pltpu.VMEM((patterns, 4 * width), f32),
            pltpu.VMEM((2 * ITERS, 4, patterns, width), f32),
            pltpu.VMEM((2 * ITERS, 4, patterns, width), f32),
            pltpu.VMEM((4, 2 * prims, width), f32),
            pltpu.VMEM((4, 2 * prims, width), f32),
            pltpu.VMEM((wides, owned, order), f32),
            pltpu.VMEM((order, order), f32),
            pltpu.VMEM((order, 4 * width), f32),
            pltpu.VMEM((5 * prims, 4 * width), f32),
            pltpu.VMEM((5 * group * prims, order if devices == group else LANES), bf16),
            pltpu.VMEM((rhs, 3 * patterns), bf16),
            pltpu.VMEM((2, order, 8 * width), bf16),
            pltpu.VMEM((4, order, width), f32),
            pltpu.VMEM((4, order, width), f32),
            pltpu.VMEM((2, order, 4 * width), bf16),
            pltpu.VMEM((4, order, width), f32),
            pltpu.VMEM((4, order, width), f32),
            pltpu.VMEM((ITERS, devices, 1, LANES), f32),
            pltpu.VMEM((group, -(-5 * prims * patterns // LANES), LANES), f32),
            pltpu.VMEM((group, prims // 2, LANES), f32),
            pltpu.SemaphoreType.REGULAR((3,)),
            dma((6,)),
            dma((2, 4)),
            dma((2 * ITERS, 4)),
            dma((2 * ITERS, 4)),
            dma((4,)),
            dma((4,)),
            dma((4,)),
            dma((4,)),
            dma((4,)),
            dma((4,)),
            dma((wides,)),
            dma((wides,)),
            dma((ITERS + 1,)),
            dma((ITERS + 1,)),
        ],
        compiler_params=pltpu.CompilerParams(
            collective_id=0, has_side_effects=True, vmem_limit_bytes=VMEM_LIMIT
        ),
        name="bddc",
    )(
        face_order.reshape(4),
        corner_map.reshape(prims),
        load_table.reshape(patterns * 4, width),
        coarse_basis.reshape(prims * 4, width),
        coarse_inverse,
        load_column.reshape(1, rhs),
        schur.reshape(4, width, inner),
        neumann.reshape(4, width, inner),
    )
    return result.reshape(1, 1, 4, rhs, width)


def solution(mesh):
    in_specs = (
        P("sub", "wide", None, None, None),
        P(),
        P("sub", "wide", None),
        P("sub", "wide", None, None),
        P("sub", "wide", None, None),
        P("sub", "wide", None, None, None),
        P("sub", "wide", None),
        P("wide", None),
    )
    out_specs = P("sub", "wide", None, None, None)
    return jax.shard_map(body, mesh=mesh, in_specs=in_specs, out_specs=out_specs, check_vma=False)
```
